32 devices in a mesh: dp: 4 (over x, core), mp: 8 (over z, y).
Axes of the slice: x: 2, y: 2, z: 4, core: 2. Of those that a mesh axis runs over, the one named last changes fastest.
Arguments:
- block_input: bfloat16 [4096, 2048], P(('dp', 'mp')), may hold values from -6 to 6
- out_cotangent: bfloat16 [4096, 2048], P(('dp', 'mp')), may hold values from -6 to 6
- segments: int32 [4, 1024], P('dp'), may hold values from 0 to 3, never falling along the last dimension, each value on 1 to 512 neighbouring positions
- domain_tags: int32 [4], P('dp'), may hold values from 0 to 7
- counts: int32 [8], replicated, may hold values from 1 to 4
- attn_gain: float32 [2048], replicated, may hold values from 0.5 to 1.5
- mlp_gain: float32 [2048], replicated, may hold values from 0.5 to 1.5
- norm_gain: float32 [2048], P('mp'), may hold values from 0.5 to 1.5
- bound_table: float32 [24, 2048], P(None, 'mp'), may hold values from -4 to 4
- w_input: bfloat16 [2048, 2048], P(None, 'mp'), may hold values from -0.125 to 0.125
- w_forget: bfloat16 [2048, 2048], P(None, 'mp'), may hold values from -0.125 to 0.125
- w_gate_mix: bfloat16 [2048, 2048], P(None, 'mp'), may hold values from -0.125 to 0.125
- w_out: bfloat16 [2048, 2048], P('mp'), may hold values from -0.1875 to 0.1875
- w_glu_gate: bfloat16 [2048, 5632], P(None, 'mp'), may hold values from -0.125 to 0.125
- w_glu_up: bfloat16 [2048, 5632], P(None, 'mp'), may hold values from -0.125 to 0.125
- w_glu_down: bfloat16 [5632, 2048], P('mp'), may hold values from -0.109375 to 0.109375
Outputs:
- result: bfloat16 [4096, 2048], P(('dp', 'mp'))
- grad_block_input: float32 [4096, 2048], P(('dp', 'mp'))
- grad_attn_gain: float32 [2048], replicated
- grad_mlp_gain: float32 [2048], replicated
- grad_norm_gain: float32 [2048], replicated
- grad_bound_table: float32 [24, 2048], replicated
- grad_input: float32 [2048, 2048], P('dp', 'mp')
- grad_forget: float32 [2048, 2048], P('dp', 'mp')
- grad_gate_mix: float32 [2048, 2048], P('dp', 'mp')
- grad_out: float32 [2048, 2048], P('mp', 'dp')
- grad_glu_gate: float32 [2048, 5632], P('dp', 'mp')
- grad_glu_up: float32 [2048, 5632], P('dp', 'mp')
- grad_glu_down: float32 [5632, 2048], P('mp', 'dp')
The draws below stay inside these ranges and needn't reach their ends.
Inputs may be any that keep to these rules, and one draw needn't show every extreme that they name: `segments`: along each row the document ids never fall; each document has at least one position.
All inputs are finite; a program needn't handle non-finite values.
Results may differ from the reference program's by a relative error of at most 0.022.
Values may be sent and summed in bfloat16 or wider, within the bound.
No kernel may reach another device: no remote copies, remote signals or barrier semaphores. Data moves between devices by JAX's collectives and lax.ppermute only.
A program may use at most 320 MiB of HBM per device.

```python
import math
import jax
import jax.numpy as jnp
import numpy as np
from jax import lax

D = 2048
FF = 5632
NLAYER = 24
LAYER = 20
LEN = 1024
NDOM = 8
SEQS = 4
TOKENS = 4096


def plant(array, rng, least, high):
    index_at = [jax.random.randint(jax.random.fold_in(rng, axis), (), 0, length) for axis, length in enumerate(array.shape)]
    main_axis = array.shape.index(max(array.shape))
    beside = index_at[:main_axis] + [(index_at[main_axis] + 1) % array.shape[main_axis]] + index_at[main_axis + 1:]
    return array.at[tuple(index_at)].set(least).at[tuple(beside)].set(high)


def shard_levels(own_key, shape, cuts, smallest, largest):
    gain, own = 1.0, jax.random.fold_in(own_key, 6)
    for dim, shards_of in cuts:
        draws = jnp.exp(jax.random.uniform(jax.random.fold_in(own, dim), (shards_of,), jnp.float32, smallest / len(cuts), largest / len(cuts)))
        gain = gain * jnp.repeat(draws, shape[dim] // shards_of).reshape([-1 if axis == dim else 1 for axis in range(len(shape))])
    return gain


def profile(count, total, most, slope):
    portions = [(1 << 20) // math.isqrt(grade ** slope) + 1 for grade in range(2, count + 1)]
    surplus, holding = total - most - (count - 1), [1] * (count - 1)
    while surplus > 0:
        free = [i for i in range(count - 1) if holding[i] < most]
        pool, budget = sum([portions[i] for i in free]), surplus
        for i in free:
            more = min(most - holding[i], max(1, budget * portions[i] // pool), surplus)
            holding[i] = holding[i] + more
            surplus = surplus - more
    return np.array([most] + holding)


def uneven_parts(key, count, total, most, skew):
    if count == 2:
        one = jax.random.randint(key, (), max(1, total - most), min(most, total - 1) + 1)
        return jnp.stack([one, total - one])
    sizes = jnp.asarray(profile(count, total, most, skew), jnp.int32)
    pairs = (count - 1) // 2
    donor, taker = sizes[1:1 + 2 * pairs:2], sizes[2:2 + 2 * pairs:2]
    margin = jnp.minimum(donor - 1, most - taker)
    passed = jax.random.randint(jax.random.fold_in(key, 1), (pairs,), 0, 1 << 20) % (margin + 1)
    sizes = sizes.at[1:1 + 2 * pairs:2].set(donor - passed).at[2:2 + 2 * pairs:2].set(taker + passed)
    return sizes[jax.random.permutation(jax.random.fold_in(key, 2), count)]


def gaussian(own_key, dims, deviation, reach, cuts=(), held_as=jnp.bfloat16):
    entries = deviation * jax.random.normal(own_key, dims, jnp.float32)
    if cuts:
        entries = entries * shard_levels(own_key, dims, cuts, -0.22, 0.18)
    return jnp.clip(entries, -reach, reach).astype(held_as)


def setup_inputs(seed: int = 0) -> dict:
    arg_keys = jax.random.split(jax.random.key(seed), 17)
    block_input = gaussian(arg_keys[0], (TOKENS, D), 1.0, 6.0, ((0, 32),))
    out_cotangent = gaussian(arg_keys[1], (TOKENS, D), 1.0, 6.0, ((0, 32),))
    segments = jax.vmap(lambda own: jnp.searchsorted(jnp.cumsum(uneven_parts(own, 4, LEN, LEN // 2, 0)), jnp.arange(LEN), side="right"))(jax.random.split(arg_keys[2], SEQS)).reshape((SEQS, LEN)).astype(jnp.int32)
    domain_tags = plant(jax.random.randint(arg_keys[3], (SEQS,), 0, NDOM), jax.random.fold_in(arg_keys[3], 1), 0, NDOM - 1).astype(jnp.int32)
    counts = plant(jax.random.randint(arg_keys[4], (NDOM,), 1, 5), jax.random.fold_in(arg_keys[4], 1), 1, 4).astype(jnp.int32)
    attn_gain = jnp.clip(1.0 + 0.1 * jax.random.normal(arg_keys[5], (D,), jnp.float32), 0.5, 1.5)
    mlp_gain = jnp.clip(1.0 + 0.1 * jax.random.normal(arg_keys[6], (D,), jnp.float32), 0.5, 1.5)
    norm_gain = jnp.clip(1.0 + 0.1 * jax.random.normal(arg_keys[7], (D,), jnp.float32), 0.5, 1.5)
    bound_table = gaussian(arg_keys[8], (NLAYER, D), 1.0, 4.0, ((1, 8),), jnp.float32)
    w_input = gaussian(arg_keys[9], (D, D), D ** -0.5, 0.125, ((1, 8),))
    w_forget = gaussian(arg_keys[10], (D, D), D ** -0.5, 0.125, ((1, 8),))
    w_gate_mix = gaussian(arg_keys[11], (D, D), D ** -0.5, 0.125, ((1, 8),))
    w_out = gaussian(arg_keys[12], (D, D), (D // 2) ** -0.5, 0.1875, ((0, 8),))
    w_glu_gate = gaussian(arg_keys[13], (D, FF), D ** -0.5, 0.125, ((1, 8),))
    w_glu_up = gaussian(arg_keys[14], (D, FF), D ** -0.5, 0.125, ((1, 8),))
    w_glu_down = gaussian(arg_keys[15], (FF, D), (FF // 2) ** -0.5, 0.109375, ((0, 8),))
    return {"block_input": block_input, "out_cotangent": out_cotangent, "segments": segments, "domain_tags": domain_tags, "counts": counts, "attn_gain": attn_gain, "mlp_gain": mlp_gain, "norm_gain": norm_gain, "bound_table": bound_table, "w_input": w_input, "w_forget": w_forget, "w_gate_mix": w_gate_mix, "w_out": w_out, "w_glu_gate": w_glu_gate, "w_glu_up": w_glu_up, "w_glu_down": w_glu_down}


EPS = 1e-06
HIGH = lax.Precision.HIGHEST

@jax.custom_vjp
def low(v):
    return lax.optimization_barrier(v.astype(jnp.bfloat16)).astype(jnp.float32)

@jax.custom_vjp
def low_back(v):
    return v

def low_keep(v):
    return (low(v), None)

def low_pass(kept, grad):
    return (grad,)

def back_keep(v):
    return (v, None)

def back_low(kept, grad):
    return (low(grad),)
low.defvjp(low_keep, low_pass)
low_back.defvjp(back_keep, back_low)

def matmul(left, right):
    return jnp.dot(left, right, precision=HIGH, preferred_element_type=jnp.float32)

def rms_scale(rows):
    return lax.rsqrt(lax.optimization_barrier(jnp.mean(rows * rows, axis=-1, keepdims=True)) + EPS)

def sequence_forward(params, rows, keep):
    attn_gain, mlp_gain, norm_gain, bound_table, w_input, w_forget, w_gate_mix, w_out, w_glu_gate, w_glu_up, w_glu_down = params
    normed = low(rows * rms_scale(rows) * attn_gain)
    pre_i = low_back(matmul(normed, w_input))
    pre_f = low_back(matmul(normed, w_forget))
    pre_g = low_back(matmul(normed, w_gate_mix))
    shares = jax.nn.softmax(bound_table, axis=0)
    bound = lax.optimization_barrier(jnp.sum(shares[1:LAYER + 1], axis=0))
    forget = bound + (1.0 - bound) * jax.nn.sigmoid(pre_f)
    update = jax.nn.silu(pre_i) * (1.0 - forget)

    def advance(state, inputs):
        decay, fresh = inputs
        state = decay * state + fresh
        return (state, state)
    _, states = lax.scan(advance, jnp.zeros((rows.shape[1],), jnp.float32), (forget * keep[:, None], update))
    gated = low(states * rms_scale(states) * norm_gain * jax.nn.silu(pre_g))
    middle = rows + low_back(matmul(gated, w_out))
    normed_two = low(middle * rms_scale(middle) * mlp_gain)
    gate = low_back(matmul(normed_two, w_glu_gate))
    up = low_back(matmul(normed_two, w_glu_up))
    hidden = low(jax.nn.silu(gate) * up)
    return middle + low_back(matmul(hidden, w_glu_down))

def reference(block_input, out_cotangent, segments, domain_tags, counts, attn_gain, mlp_gain, norm_gain, bound_table, w_input, w_forget, w_gate_mix, w_out, w_glu_gate, w_glu_up, w_glu_down):
    params = tuple((p.astype(jnp.float32) for p in (attn_gain, mlp_gain, norm_gain, bound_table, w_input, w_forget, w_gate_mix, w_out, w_glu_gate, w_glu_up, w_glu_down)))
    rows_all = block_input.astype(jnp.float32).reshape(SEQS, LEN, D)
    cot_all = out_cotangent.astype(jnp.float32).reshape(SEQS, LEN, D)
    keep_all = jnp.concatenate([jnp.zeros((SEQS, 1), jnp.float32), (segments[:, 1:] == segments[:, :-1]).astype(jnp.float32)], axis=1)
    seq_weight = lax.rsqrt(counts[domain_tags].astype(jnp.float32))

    def one(total, item):
        rows, cot, keep, weight = item
        out, pull = jax.vjp(lambda p, r: sequence_forward(p, r, keep), params, rows)
        grads, grad_rows = pull(cot * weight)
        total = jax.tree.map(jnp.add, total, grads)
        return (total, (out.astype(jnp.bfloat16), grad_rows))
    start = jax.tree.map(jnp.zeros_like, params)
    total, (outs, grad_rows) = lax.scan(one, start, (rows_all, cot_all, keep_all, seq_weight))
    g_attn, g_mlp, g_norm, g_table, g_in, g_forget, g_gate, g_out, g_glu_gate, g_glu_up, g_glu_down = total
    return (outs.reshape(TOKENS, D), grad_rows.reshape(TOKENS, D), g_attn, g_mlp, g_norm, g_table, g_in, g_forget, g_gate, g_out, g_glu_gate, g_glu_up, g_glu_down)
```

```python
import functools

import jax
import jax.numpy as jnp
import numpy as np
from jax import lax
from jax.experimental import pallas as pl
from jax.experimental.pallas import tpu as pltpu
from jax.sharding import PartitionSpec as P

NLAYER = 24
LAYER = 20
LEN = 1024
NDOM = 8
EXT = 128
STEP = 32
EPS = 1e-06
F32 = jnp.float32
BF16 = jnp.bfloat16
MIB = 1 << 20


def vmem():
    return pl.BlockSpec(memory_space=pltpu.VMEM)


def smem():
    return pl.BlockSpec(memory_space=pltpu.SMEM)


def params(limit=48):
    return pltpu.CompilerParams(vmem_limit_bytes=limit * MIB)


def cost(flops, nbytes, trans=0):
    return pl.CostEstimate(flops=flops, bytes_accessed=nbytes, transcendentals=trans)


def inverse_rms(rows):
    return lax.rsqrt(jnp.mean(rows * rows, axis=1, keepdims=True) + EPS)


def two_terms(value):
    high = value.astype(BF16)
    return high, (value - high.astype(F32)).astype(BF16)


def forward_kernel(
    nat_ref, slot_ref, pre_a, pre_b, pre_c, keep_ref, bound_ref, gain_ref, wout_ref,
    state_ref, prior_ref, part_ref, decay_s, fresh_s, gated_s, prod_s, last_s, carry_s,
    *, blk,
):
    chans = bound_ref.shape[1]
    total, width = part_ref.shape[0], part_ref.shape[1] - EXT
    nblk = total // blk
    per = blk // STEP
    tiles = range(chans // 128)
    base = 0
    for pre_ref in (pre_a, pre_b, pre_c):

        def gates(step, _, pre_ref=pre_ref, base=base):
            row = pl.multiple_of(step * STEP, STEP)
            slot = base // blk + step // per
            at = pl.multiple_of(nat_ref[slot] * blk + (step % per) * STEP, STEP)
            out = pl.ds(pl.multiple_of(base + row, STEP), STEP)
            keep = keep_ref[pl.ds(at, STEP), :]
            for tile in tiles:
                lo = tile * 128
                bound = bound_ref[:, lo : lo + 128]
                pre_i = pre_ref[pl.ds(row, STEP), lo : lo + 128]
                pre_f = pre_ref[pl.ds(row, STEP), chans + lo : chans + lo + 128]
                forget = bound + (1.0 - bound) * jax.nn.sigmoid(pre_f)
                decay_s[tile, out, :] = forget * keep
                fresh_s[tile, out, :] = jax.nn.silu(pre_i) * (1.0 - forget)
            return 0

        lax.fori_loop(0, pre_ref.shape[0] // STEP, gates, 0)
        base += pre_ref.shape[0]

    def local(pos, carried):
        rows = pl.ds(pos, nblk, stride=blk)
        after = []
        for tile, (prod, last) in enumerate(carried):
            decay = decay_s[tile, rows, :]
            after.append((prod * decay, decay * last + fresh_s[tile, rows, :]))
        return after

    shape = (nblk, 128)
    ends = lax.fori_loop(
        0, blk, local, [(jnp.ones(shape, F32), jnp.zeros(shape, F32)) for _ in tiles], unroll=8
    )
    for tile, (prod, last) in enumerate(ends):
        prod_s[tile] = prod
        last_s[tile] = last

    def link(block, carry):
        own = pl.ds(slot_ref[block], 1)
        after = []
        for tile in tiles:
            carry_s[tile, own, :] = carry[tile]
            after.append(prod_s[tile, own, :] * carry[tile] + last_s[tile, own, :])
        return after

    lax.fori_loop(0, nblk, link, [jnp.zeros((1, 128), F32) for _ in tiles])

    def scan(pos, states):
        rows = pl.ds(pos, nblk, stride=blk)
        after = []
        for tile in tiles:
            prior_ref[tile, rows, :] = states[tile]
            state = decay_s[tile, rows, :] * states[tile] + fresh_s[tile, rows, :]
            state_ref[tile, rows, :] = state
            after.append(state)
        return after

    lax.fori_loop(0, blk, scan, [carry_s[tile] for tile in tiles], unroll=8)
    base = 0
    for pre_ref in (pre_a, pre_b, pre_c):

        def gate(step, _, pre_ref=pre_ref, base=base):
            row = pl.multiple_of(step * STEP, STEP)
            out = pl.ds(pl.multiple_of(base + row, STEP), STEP)
            square = jnp.zeros((STEP, 1), F32)
            for tile in tiles:
                lo = tile * 128
                state = state_ref[tile, out, :]
                pre_g = pre_ref[pl.ds(row, STEP), 2 * chans + lo : 2 * chans + lo + 128]
                gated = state * gain_ref[:, lo : lo + 128] * jax.nn.silu(pre_g)
                gated_s[out, lo : lo + 128] = gated.astype(BF16)
                square += jnp.sum(state * state, axis=1, keepdims=True)
            high, low = two_terms(square)
            lane = lax.broadcasted_iota(jnp.int32, (STEP, EXT), 1)
            part_ref[out, width:] = jnp.where(
                lane == 0, high.astype(F32), jnp.where(lane == 1, low.astype(F32), 0.0)
            ).astype(BF16)
            return 0

        lax.fori_loop(0, pre_ref.shape[0] // STEP, gate, 0)
        base += pre_ref.shape[0]

    tile = 256

    def project(step, _):
        cols = pl.ds(pl.multiple_of(step * tile, tile), tile)
        part_ref[:, cols] = jnp.dot(
            gated_s[...], wout_ref[:, cols], preferred_element_type=F32
        ).astype(BF16)
        return 0

    lax.fori_loop(0, width // tile, project, 0)


def recur_forward(nat, slot, pres, keep, bound, gain, w_out, blk):
    chans, width = w_out.shape
    total = sum(pre.shape[0] for pre in pres)
    nblk = total // blk
    tiles = chans // 128
    out = jax.ShapeDtypeStruct
    return pl.pallas_call(
        functools.partial(forward_kernel, blk=blk),
        out_shape=(
            out((tiles, total, 128), F32),
            out((tiles, total, 128), F32),
            out((total, width + EXT), BF16),
        ),
        in_specs=[smem(), smem()] + [vmem()] * 7,
        out_specs=(vmem(),) * 3,
        scratch_shapes=[
            pltpu.VMEM((tiles, total, 128), F32),
            pltpu.VMEM((tiles, total, 128), F32),
            pltpu.VMEM((total, chans), BF16),
            pltpu.VMEM((tiles, nblk, 128), F32),
            pltpu.VMEM((tiles, nblk, 128), F32),
            pltpu.VMEM((tiles, nblk, 128), F32),
        ],
        compiler_params=params(),
        cost_estimate=cost(
            2 * total * chans * width, total * (chans * 20 + width * 2), total * chans * 6
        ),
        name="recur_forward",
    )(nat, slot, *pres, keep, bound, gain, w_out)


def backward_kernel(
    nat_ref, slot_ref, grad_a, grad_b, grad_c, pre_a, pre_b, pre_c, state_ref, prior_ref,
    ext_ref, keep_ref, bound_ref, gain_ref,
    gpre_ref, gated_ref, gain_sum_ref, bound_sum_ref,
    decay_s, grad_s, prod_s, last_s, carry_s,
    *, blk, width,
):
    chans = bound_ref.shape[1]
    total = gated_ref.shape[0]
    nblk = total // blk
    per = blk // STEP
    tiles = range(chans // 128)
    zero_row = jnp.zeros((1, 128), F32)
    base = 0
    sums = [zero_row for _ in tiles]
    for grad_ref, pre_ref in ((grad_a, pre_a), (grad_b, pre_b), (grad_c, pre_c)):

        def enter(step, summed, grad_ref=grad_ref, pre_ref=pre_ref, base=base):
            row = pl.multiple_of(step * STEP, STEP)
            slot = base // blk + step // per
            at = pl.multiple_of(nat_ref[slot] * blk + (step % per) * STEP, STEP)
            out = pl.ds(pl.multiple_of(base + row, STEP), STEP)
            here = pl.ds(row, STEP)
            ext = ext_ref[out, :].astype(F32)
            inner = (ext[:, 0:1] + ext[:, 1:2]) * (1.0 / width)
            inv = ext[:, 2:3] + ext[:, 3:4]
            keep = keep_ref[pl.ds(at, STEP), :]
            after = []
            for tile in tiles:
                lo = tile * 128
                bound = bound_ref[:, lo : lo + 128]
                gain = gain_ref[:, lo : lo + 128]
                grad = grad_ref[here, lo : lo + 128]
                pre_f = pre_ref[here, chans + lo : chans + lo + 128]
                pre_g = pre_ref[here, 2 * chans + lo : 2 * chans + lo + 128]
                unit = state_ref[tile, out, :] * inv
                sig_g = jax.nn.sigmoid(pre_g)
                act_g = pre_g * sig_g
                scaled = gain * act_g
                grad_s[tile, out, :] = inv * (grad * scaled - unit * inner)
                gated_ref[out, lo : lo + 128] = (unit * scaled).astype(BF16)
                both = grad * unit
                slope = sig_g * (1.0 + pre_g * (1.0 - sig_g))
                gpre_ref[out, 2 * chans + lo : 2 * chans + lo + 128] = (
                    both * gain * slope
                ).astype(BF16)
                forget = bound + (1.0 - bound) * jax.nn.sigmoid(pre_f)
                decay_s[tile, out, :] = forget * keep
                after.append(summed[tile] + jnp.sum(both * act_g, axis=0, keepdims=True))
            return after

        sums = lax.fori_loop(0, pre_ref.shape[0] // STEP, enter, sums)
        base += pre_ref.shape[0]
    for tile in tiles:
        gain_sum_ref[:, tile * 128 : tile * 128 + 128] = sums[tile]

    def local(step, carried):
        rows = pl.ds(blk - 1 - step, nblk, stride=blk)
        after = []
        for tile, (prod, last) in enumerate(carried):
            decay = decay_s[tile, rows, :]
            after.append((prod * decay, decay * (grad_s[tile, rows, :] + last)))
        return after

    shape = (nblk, 128)
    ends = lax.fori_loop(
        0, blk, local, [(jnp.ones(shape, F32), jnp.zeros(shape, F32)) for _ in tiles], unroll=8
    )
    for tile, (prod, last) in enumerate(ends):
        prod_s[tile] = prod
        last_s[tile] = last

    def link(step, carry):
        own = pl.ds(slot_ref[nblk - 1 - step], 1)
        after = []
        for tile in tiles:
            carry_s[tile, own, :] = carry[tile]
            after.append(prod_s[tile, own, :] * carry[tile] + last_s[tile, own, :])
        return after

    lax.fori_loop(0, nblk, link, [zero_row for _ in tiles])

    def scan(step, carried):
        rows = pl.ds(blk - 1 - step, nblk, stride=blk)
        after = []
        for tile in tiles:
            grad = grad_s[tile, rows, :] + carried[tile]
            grad_s[tile, rows, :] = grad
            after.append(decay_s[tile, rows, :] * grad)
        return after

    lax.fori_loop(0, blk, scan, [carry_s[tile] for tile in tiles], unroll=8)
    base = 0
    sums = [zero_row for _ in tiles]
    for pre_ref in (pre_a, pre_b, pre_c):

        def leave(step, summed, pre_ref=pre_ref, base=base):
            row = pl.multiple_of(step * STEP, STEP)
            slot = base // blk + step // per
            at = pl.multiple_of(nat_ref[slot] * blk + (step % per) * STEP, STEP)
            out = pl.ds(pl.multiple_of(base + row, STEP), STEP)
            here = pl.ds(row, STEP)
            keep = keep_ref[pl.ds(at, STEP), :]
            after = []
            for tile in tiles:
                lo = tile * 128
                bound = bound_ref[:, lo : lo + 128]
                pre_i = pre_ref[here, lo : lo + 128]
                pre_f = pre_ref[here, chans + lo : chans + lo + 128]
                grad = grad_s[tile, out, :]
                sig_i = jax.nn.sigmoid(pre_i)
                sig_f = jax.nn.sigmoid(pre_f)
                forget = bound + (1.0 - bound) * sig_f
                rest = 1.0 - sig_f
                grad_forget = grad * keep * prior_ref[tile, out, :] - grad * (pre_i * sig_i)
                grad_i = grad * (1.0 - forget) * (sig_i * (1.0 + pre_i * (1.0 - sig_i)))
                gpre_ref[out, lo : lo + 128] = grad_i.astype(BF16)
                grad_f = grad_forget * (1.0 - bound) * sig_f * rest
                gpre_ref[out, chans + lo : chans + lo + 128] = grad_f.astype(BF16)
                after.append(summed[tile] + jnp.sum(grad_forget * rest, axis=0, keepdims=True))
            return after

        sums = lax.fori_loop(0, pre_ref.shape[0] // STEP, leave, sums)
        base += pre_ref.shape[0]
    for tile in tiles:
        bound_sum_ref[:, tile * 128 : tile * 128 + 128] = sums[tile]


def recur_backward(nat, slot, grads, pres, state, prior, ext, keep, bound, gain, blk, width):
    tiles, total, _ = state.shape
    chans = tiles * 128
    nblk = total // blk
    out = jax.ShapeDtypeStruct
    return pl.pallas_call(
        functools.partial(backward_kernel, blk=blk, width=width),
        out_shape=(
            out((total, 3 * chans), BF16),
            out((total, chans), BF16),
            out((1, chans), F32),
            out((1, chans), F32),
        ),
        in_specs=[smem(), smem()] + [vmem()] * 12,
        out_specs=(vmem(),) * 4,
        scratch_shapes=[
            pltpu.VMEM((tiles, total, 128), F32),
            pltpu.VMEM((tiles, total, 128), F32),
            pltpu.VMEM((tiles, nblk, 128), F32),
            pltpu.VMEM((tiles, nblk, 128), F32),
            pltpu.VMEM((tiles, nblk, 128), F32),
        ],
        compiler_params=params(),
        cost_estimate=cost(total * chans * 60, total * chans * 36, total * chans * 8),
        name="recur_backward",
    )(nat, slot, *grads, *pres, state, prior, ext, keep, bound, gain)


def middle_kernel(r_ref, l_ref, part_ref, rows_ref, gain_ref, normed_ref, middle_ref, inv_ref):
    width = rows_ref.shape[1]
    gain = gain_ref[...]

    def chunk(step, _):
        rows = pl.ds(pl.multiple_of(step * 16, 16), 16)
        summed = (
            r_ref[rows, :].astype(F32) + l_ref[rows, :].astype(F32) + part_ref[rows, :].astype(F32)
        )
        square = summed[:, width : width + 1] + summed[:, width + 1 : width + 2]
        inv = lax.rsqrt(square / width + EPS)
        middle = rows_ref[rows, :].astype(F32) + summed[:, :width] * inv
        inv_two = inverse_rms(middle)
        middle_ref[rows, :] = middle
        normed_ref[rows, :] = (middle * inv_two * gain).astype(BF16)
        lane = lax.broadcasted_iota(jnp.int32, (16, EXT), 1)
        inv_ref[rows, :] = jnp.where(lane == 0, inv, jnp.where(lane == 1, inv_two, 0.0))
        return 0

    lax.fori_loop(0, rows_ref.shape[0] // 16, chunk, 0)


def make_middle(r_in, l_in, part, rows, gain):
    blk, width = rows.shape
    out = jax.ShapeDtypeStruct
    return pl.pallas_call(
        middle_kernel,
        grid=(1,),
        out_shape=(out((blk, width), BF16), out((blk, width), F32), out((blk, EXT), F32)),
        in_specs=[
            vmem(),
            vmem(),
            pl.BlockSpec((blk, width + EXT), lambda i: (0, 0)),
            vmem(),
            vmem(),
        ],
        out_specs=(vmem(),) * 3,
        compiler_params=params(),
        cost_estimate=cost(blk * width * 12, blk * width * 14),
        name="make_middle",
    )(r_in, l_in, part, rows, gain)


def middle_grad_kernel(
    r_ref, l_ref, part_ref, rows_ref, middle_ref, inv_ref, cot_ref, weight_ref, gain_ref,
    grad_ref, send_ref, gain_sum_ref,
):
    blk, width = rows_ref.shape
    gain = gain_ref[...]
    weight = weight_ref[0, 0]

    def chunk(step, summed):
        rows = pl.ds(pl.multiple_of(step * 16, 16), 16)
        grad_two = (
            r_ref[rows, :].astype(F32) + l_ref[rows, :].astype(F32) + part_ref[rows, :].astype(F32)
        )
        inv = inv_ref[rows, :]
        inv_mix, inv_two = inv[:, 0:1], inv[:, 1:2]
        middle = middle_ref[rows, :]
        unit = middle * inv_two
        scaled = grad_two * gain
        mean = jnp.mean(scaled * unit, axis=1, keepdims=True)
        grad = cot_ref[rows, :].astype(F32) * weight + inv_two * (scaled - unit * mean)
        grad_ref[rows, :] = grad
        sent = grad.astype(BF16)
        send_ref[rows, :width] = sent
        mix = middle - rows_ref[rows, :].astype(F32)
        inner = jnp.sum(sent.astype(F32) * mix, axis=1, keepdims=True)
        high, low = two_terms(inner)
        inv_high, inv_low = two_terms(inv_mix)
        lane = lax.broadcasted_iota(jnp.int32, (16, EXT), 1)
        ext = jnp.where(
            lane == 0,
            high.astype(F32),
            jnp.where(
                lane == 1,
                low.astype(F32),
                jnp.where(
                    lane == 2,
                    inv_high.astype(F32),
                    jnp.where(lane == 3, inv_low.astype(F32), 0.0),
                ),
            ),
        )
        send_ref[rows, width:] = ext.astype(BF16)
        return summed + jnp.sum(grad_two * unit, axis=0, keepdims=True)

    gain_sum_ref[...] = lax.fori_loop(0, blk // 16, chunk, jnp.zeros((1, width), F32))


def make_middle_grad(r_in, l_in, part, rows, middle, inv, cot, weight, gain):
    blk, width = rows.shape
    out = jax.ShapeDtypeStruct
    return pl.pallas_call(
        middle_grad_kernel,
        grid=(1,),
        out_shape=(
            out((blk, width), F32),
            out((blk, width + EXT), BF16),
            out((1, width), F32),
        ),
        in_specs=[vmem(), vmem(), pl.BlockSpec((blk, width), lambda i: (0, 0))]
        + [vmem()] * 4
        + [smem(), vmem()],
        out_specs=(vmem(),) * 3,
        compiler_params=params(),
        cost_estimate=cost(blk * width * 16, blk * width * 20),
        name="make_middle_grad",
    )(r_in, l_in, part, rows, middle, inv, cot, weight, gain)


def input_grad_kernel(r_ref, l_ref, part_ref, rows_ref, grad_ref, gain_ref, out_ref):
    gain = gain_ref[...]

    def chunk(step, _):
        rows = pl.ds(pl.multiple_of(step * 16, 16), 16)
        grad = (
            r_ref[rows, :].astype(F32) + l_ref[rows, :].astype(F32) + part_ref[rows, :].astype(F32)
        )
        own = rows_ref[rows, :].astype(F32)
        inv = inverse_rms(own)
        unit = own * inv
        scaled = grad * gain
        mean = jnp.mean(scaled * unit, axis=1, keepdims=True)
        out_ref[rows, :] = grad_ref[rows, :] + inv * (scaled - unit * mean)
        return 0

    lax.fori_loop(0, rows_ref.shape[0] // 16, chunk, 0)


def make_input_grad(r_in, l_in, part, rows, grad, gain):
    blk, width = rows.shape
    return pl.pallas_call(
        input_grad_kernel,
        grid=(1,),
        out_shape=jax.ShapeDtypeStruct((blk, width), F32),
        in_specs=[vmem(), vmem(), pl.BlockSpec((blk, width), lambda i: (0, 0))] + [vmem()] * 3,
        out_specs=vmem(),
        compiler_params=params(),
        cost_estimate=cost(blk * width * 12, blk * width * 16),
        name="make_input_grad",
    )(r_in, l_in, part, rows, grad, gain)


class Ring:
    def __init__(self, size):
        self.size = size
        self.half = size // 2 - 1
        order = list(range(0, size, 2)) + list(range(size - 1, 0, -2))
        self.place = {device: at for at, device in enumerate(order)}
        self.right = [(order[i], order[(i + 1) % size]) for i in range(size)]
        self.left = [(b, a) for a, b in self.right]
        offs = [0]
        for k in range(1, self.half + 1):
            offs += [-k, k]
        offs.append(self.half + 1)
        nat = np.zeros((size, size), np.int32)
        slot = np.zeros((size, size), np.int32)
        for device in range(size):
            for at, off in enumerate(offs):
                block = order[(self.place[device] + off) % size]
                nat[device, at] = block
                slot[device, block] = at
        self.nat, self.slot = nat, slot

    def go_right(self, value):
        return lax.ppermute(value, "mp", self.right)

    def go_left(self, value):
        return lax.ppermute(value, "mp", self.left)

    def gather(self, block):
        rows = block.shape[0] // 2
        right = left = block
        blocks = [block]
        for _ in range(self.half):
            right, left = self.go_right(right), self.go_left(left)
            blocks += [right, left]
        far = [self.go_right(right[:rows]), self.go_left(left[rows:])]
        return blocks, jnp.concatenate(far, axis=0)

    def groups(self, blocks, far):
        return [
            jnp.concatenate(blocks[:-2], axis=0),
            jnp.concatenate(blocks[-2:], axis=0),
            far,
        ]

    def scatter(self, part):
        far = part(self.size - 1)
        rows = far.shape[0] // 2
        right, left = self.go_right(far[:rows]), self.go_left(far[rows:])
        for k in range(self.half, 0, -1):
            to_right, to_left = part(2 * k), part(2 * k - 1)
            if k == self.half:
                right = jnp.concatenate([add(right, to_right[:rows]), to_right[rows:]], axis=0)
                left = jnp.concatenate([to_left[:rows], add(left, to_left[rows:])], axis=0)
            else:
                right, left = add(right, to_right), add(left, to_left)
            right, left = self.go_right(right), self.go_left(left)
        return right, left


def add(a, b):
    return (a.astype(F32) + b.astype(F32)).astype(BF16)


def dp_swap(value, bit):
    return lax.ppermute(value, "dp", [(i, i ^ bit) for i in range(lax.axis_size("dp"))])


def dp_scatter(product, split, count):
    index = lax.axis_index("dp")
    size = split // count

    def own(block):
        return product(block * size, size)

    far, near = index ^ 2, index
    far_sum = own(far) + dp_swap(own(far ^ 1).astype(BF16), 1).astype(F32)
    near_sum = own(near) + dp_swap(own(near ^ 1).astype(BF16), 1).astype(F32)
    return near_sum + dp_swap(far_sum.astype(BF16), 2).astype(F32)


def dot_tn(lhs, rhs):
    return lax.dot_general(lhs, rhs, (((0,), (0,)), ((), ())), preferred_element_type=F32)


def dot_nt(lhs, rhs):
    return lax.dot_general(lhs, rhs, (((1,), (1,)), ((), ())), preferred_element_type=F32)


def dot_nn(lhs, rhs):
    return jnp.dot(lhs, rhs, preferred_element_type=F32)


def silu_slope(value):
    sig = jax.nn.sigmoid(value)
    return sig * (1.0 + value * (1.0 - sig))


def local(
    block_input,
    out_cotangent,
    segments,
    domain_tags,
    counts,
    attn_gain,
    mlp_gain,
    norm_gain,
    bound_table,
    w_input,
    w_forget,
    w_gate_mix,
    w_out,
    w_glu_gate,
    w_glu_up,
    w_glu_down,
):
    blk, width = block_input.shape
    chans = w_input.shape[1]
    seqs = segments.shape[0]
    total = seqs * LEN
    mp_size, dp_size = lax.axis_size("mp"), lax.axis_size("dp")
    mp_index = lax.axis_index("mp")
    ring = Ring(mp_size)
    nat = lax.dynamic_index_in_dim(jnp.asarray(ring.nat), mp_index, 0, keepdims=False)
    slot = lax.dynamic_index_in_dim(jnp.asarray(ring.slot), mp_index, 0, keepdims=False)

    lanes = -(-chans // 128) * 128
    pad = lanes - chans

    def pad_cols(array):
        return jnp.pad(array, ((0, 0), (0, pad))) if pad else array

    own_rows = block_input.astype(F32)
    normed = (own_rows * inverse_rms(own_rows) * attn_gain).astype(BF16)
    normed_blocks, normed_far = ring.gather(normed)
    normed_groups = ring.groups(normed_blocks, normed_far)

    w_mix = jnp.concatenate([pad_cols(w_input), pad_cols(w_forget), pad_cols(w_gate_mix)], axis=1)
    w_out_pad = jnp.pad(w_out, ((0, pad), (0, 0))) if pad else w_out
    shares = jax.nn.softmax(bound_table, axis=0)
    layer_ids = jnp.arange(NLAYER)
    pick = ((layer_ids >= 1) & (layer_ids <= LAYER)).astype(F32)[:, None]
    bound = pad_cols(jnp.sum(shares * pick, axis=0)[None, :])
    gain = pad_cols(norm_gain[None, :])
    keep = jnp.concatenate(
        [jnp.zeros((seqs, 1), F32), (segments[:, 1:] == segments[:, :-1]).astype(F32)], axis=1
    ).reshape(total, 1)

    seq_count = jnp.sum(
        jnp.where(
            domain_tags[:, None] == jnp.arange(NDOM)[None, :], counts.astype(F32)[None, :], 0.0
        ),
        axis=1,
    )
    weight = lax.dynamic_slice_in_dim(lax.rsqrt(seq_count), mp_index * blk // LEN, 1, 0)
    grad_b = (out_cotangent.astype(F32) * weight[:, None]).astype(BF16)
    cot_blocks, cot_far = ring.gather(grad_b)
    grad_all = jnp.concatenate(cot_blocks + [cot_far], axis=0)

    pres = [dot_nn(group, w_mix) for group in normed_groups]
    state, prior, part = recur_forward(nat, slot, pres, keep, bound, gain, w_out_pad, blk)

    def rows_of(array):
        return lambda at: lax.slice_in_dim(array, at * blk, (at + 1) * blk, axis=0)

    right, left = ring.scatter(rows_of(part))
    normed_two, middle, invs = make_middle(right, left, part, block_input, mlp_gain[None, :])

    two_blocks, two_far = ring.gather(normed_two)
    grad_hidden = dot_nt(grad_all, w_glu_down)
    hidden, grad_gate, grad_up = [], [], []
    start = 0
    for group in ring.groups(two_blocks, two_far):
        gate, up = dot_nn(group, w_glu_gate), dot_nn(group, w_glu_up)
        back = lax.slice_in_dim(grad_hidden, start, start + group.shape[0], axis=0)
        start += group.shape[0]
        sig = jax.nn.sigmoid(gate)
        act = gate * sig
        hidden.append((act * up).astype(BF16))
        grad_gate.append((back * up * (sig * (1.0 + gate * (1.0 - sig)))).astype(BF16))
        grad_up.append((back * act).astype(BF16))
    far_term = (dot_nt(grad_gate[2], w_glu_gate) + dot_nt(grad_up[2], w_glu_up)).astype(BF16)
    gate_near = jnp.concatenate(grad_gate[:2], axis=0)
    up_near = jnp.concatenate(grad_up[:2], axis=0)
    near_term = (dot_nt(gate_near, w_glu_gate) + dot_nt(up_near, w_glu_up)).astype(BF16)
    near_rows = rows_of(near_term)
    right, left = ring.scatter(lambda at: far_term if at == mp_size - 1 else near_rows(at))
    grad_middle, sent, mlp_term = make_middle_grad(
        right, left, near_term, block_input, middle, invs, out_cotangent, weight[:, None],
        mlp_gain[None, :],
    )

    sent_blocks, sent_far = ring.gather(sent)
    sent_groups = ring.groups(sent_blocks, sent_far)
    w_out_ext = jnp.pad(w_out_pad, ((0, 0), (0, EXT)))
    grads = [dot_nt(group, w_out_ext) for group in sent_groups]
    sent_all = jnp.concatenate(sent_groups, axis=0)
    grad_pre, gated, norm_term, bound_grad = recur_backward(
        nat, slot, grads, pres, state, prior, sent_all[:, width:], keep, bound, gain, blk, width
    )
    term = dot_nt(grad_pre, w_mix).astype(BF16)
    right, left = ring.scatter(rows_of(term))
    grad_block_input = make_input_grad(
        right, left, term, block_input, grad_middle, attn_gain[None, :]
    )

    hidden_all = jnp.concatenate(hidden, axis=0)
    out_part = dot_nn(hidden_all, w_glu_down).astype(BF16)
    right, left = ring.scatter(rows_of(out_part))
    result = (
        middle + right.astype(F32) + left.astype(F32) + rows_of(out_part)(0).astype(F32)
    ).astype(BF16)

    normed_all = jnp.concatenate(normed_groups, axis=0)
    two_all = jnp.concatenate(two_blocks + [two_far], axis=0)
    grad_gate_all = jnp.concatenate([gate_near, grad_gate[2]], axis=0)
    grad_up_all = jnp.concatenate([up_near, grad_up[2]], axis=0)

    def cols(array, at, size):
        return lax.dynamic_slice_in_dim(array, at, size, axis=1)

    def column_split(lhs, rhs):
        return dp_scatter(lambda at, size: dot_tn(cols(lhs, at, size), rhs), width, dp_size)

    def row_split(lhs, rhs):
        return dp_scatter(lambda at, size: dot_tn(lhs, cols(rhs, at, size)), width, dp_size)

    down_grad = row_split(hidden_all, grad_all)
    glu_gate_grad = column_split(two_all, grad_gate_all)
    glu_up_grad = column_split(two_all, grad_up_all)
    out_grad = row_split(gated, sent_all)[:chans]
    mix_grad = column_split(normed_all, grad_pre)

    attn_term = jnp.sum(normed_all.astype(F32) * term.astype(F32), axis=0) / attn_gain
    pick_grad = pick * bound_grad[:, :chans]
    table_term = shares * (pick_grad - jnp.sum(shares * pick_grad, axis=0, keepdims=True))
    packed = jnp.concatenate(
        [attn_term, mlp_term[0], norm_term[0, :chans], table_term.reshape(NLAYER * chans)]
    )
    packed = jnp.pad(packed, (0, -packed.size % 128)).reshape(-1, 128)
    packed = packed + dp_swap(packed, 1)
    packed = packed + dp_swap(packed, 2)
    count = packed.shape[0]
    right = left = packed
    found = [packed]
    for _ in range(ring.half):
        right, left = ring.go_right(right), ring.go_left(left)
        found += [right, left]
    found.append(ring.go_right(right))
    found = jnp.take(jnp.stack(found), slot, axis=0).reshape(mp_size, count * 128)
    summed = jnp.sum(found[:, : 2 * width], axis=0)
    attn_sum, mlp_sum = summed[:width], summed[width:]
    norm_sum = found[:, 2 * width : 2 * width + chans].reshape(mp_size * chans)
    table_sum = (
        found[:, 2 * width + chans : 2 * width + (1 + NLAYER) * chans]
        .reshape(mp_size, NLAYER, chans)
        .transpose(1, 0, 2)
        .reshape(NLAYER, mp_size * chans)
    )
    return (
        result,
        grad_block_input,
        attn_sum,
        mlp_sum,
        norm_sum,
        table_sum,
        mix_grad[:, :chans],
        mix_grad[:, lanes : lanes + chans],
        mix_grad[:, 2 * lanes : 2 * lanes + chans],
        out_grad,
        glu_gate_grad,
        glu_up_grad,
        down_grad,
    )


def solution(mesh):
    placed = (
        P(("dp", "mp"), None),
        P(("dp", "mp"), None),
        P("dp", None),
        P("dp"),
        P(),
        P(),
        P(),
        P("mp"),
        P(None, "mp"),
        P(None, "mp"),
        P(None, "mp"),
        P(None, "mp"),
        P("mp", None),
        P(None, "mp"),
        P(None, "mp"),
        P("mp", None),
    )
    return jax.shard_map(
        local,
        mesh=mesh,
        in_specs=placed,
        out_specs=(
            P(("dp", "mp"), None),
            P(("dp", "mp"), None),
            P(),
            P(),
            P(),
            P(),
            P("dp", "mp"),
            P("dp", "mp"),
            P("dp", "mp"),
            P("mp", "dp"),
            P("dp", "mp"),
            P("dp", "mp"),
            P("mp", "dp"),
        ),
        check_vma=False,
    )
```

```python
import functools

import jax
import jax.numpy as jnp
import numpy as np
from jax import lax
from jax.experimental import pallas as pl
from jax.experimental.pallas import tpu as pltpu
from jax.sharding import PartitionSpec as P

NLAYER = 24
LAYER = 20
LEN = 1024
NDOM = 8
EXT = 128
SUB = 4
GAP = 8
EPS = 1e-06
F32 = jnp.float32
BF16 = jnp.bfloat16
MIB = 1 << 20
GRANT = 0


def vmem():
    return pl.BlockSpec(memory_space=pltpu.VMEM)


def smem():
    return pl.BlockSpec(memory_space=pltpu.SMEM)


def params(arrays, least=GRANT):
    used = 0
    for shape, item in arrays:
        lead = int(np.prod(shape[:-2])) if len(shape) > 2 else 1
        used += lead * (-(-shape[-2] // 16) * 16) * (-(-shape[-1] // 128) * 128) * item
    return pltpu.CompilerParams(vmem_limit_bytes=max(used + used // 8 + 2 * MIB, least * MIB))


def tie(value, *after):
    return lax.optimization_barrier((value, *after))[0]


def cost(flops, nbytes, trans=0):
    return pl.CostEstimate(flops=flops, bytes_accessed=nbytes, transcendentals=trans)


def joined(refs):
    return refs[0][...] if len(refs) == 1 else jnp.concatenate([ref[...] for ref in refs], axis=0)


def dot_tn(lhs, rhs):
    return lax.dot_general(lhs, rhs, (((0,), (0,)), ((), ())), preferred_element_type=F32)


def dot_nt(lhs, rhs):
    return lax.dot_general(lhs, rhs, (((1,), (1,)), ((), ())), preferred_element_type=F32)


def dot_nn(lhs, rhs):
    return jnp.dot(lhs, rhs, preferred_element_type=F32)


def inverse_rms(rows):
    return lax.rsqrt(jnp.mean(rows * rows, axis=1, keepdims=True) + EPS)


def two_terms(value):
    high = value.astype(BF16)
    return high, (value - high.astype(F32)).astype(BF16)


def forward_kernel(
    nat_ref, slot_ref, keep_ref, bound_ref, gain_ref, pre_ref,
    state_ref, prior_ref, gated_ref, decay_s, fresh_s, square_s, prod_s, last_s, carry_s,
    *, blk,
):
    chans = bound_ref.shape[1]
    total = keep_ref.shape[0]
    nblk = total // blk
    tiles = range(chans // 128)

    def gates(slot, _):
        at = pl.multiple_of(nat_ref[slot] * blk, blk)
        row = pl.multiple_of(slot * blk, blk)
        out = pl.ds(pl.multiple_of(slot * (blk + GAP), 8), blk)
        keep = keep_ref[pl.ds(at, blk), :]
        for tile in tiles:
            lo = tile * 128
            bound = bound_ref[:, lo : lo + 128]
            pre_i = pre_ref[pl.ds(row, blk), lo : lo + 128]
            pre_f = pre_ref[pl.ds(row, blk), chans + lo : chans + lo + 128]
            forget = bound + (1.0 - bound) * jax.nn.sigmoid(pre_f)
            decay_s[tile, out, :] = forget * keep
            fresh_s[tile, out, :] = jax.nn.silu(pre_i) * (1.0 - forget)
        return 0

    lax.fori_loop(0, nblk, gates, 0)
    size = blk // SUB
    lanes = [(tile, sub) for tile in tiles for sub in range(SUB)]

    def local(pos, carried):
        after = []
        for (tile, sub), (prod, last) in zip(lanes, carried):
            rows = pl.ds(sub * size + pos, nblk, stride=blk + GAP)
            decay = decay_s[tile, rows, :]
            after.append((prod * decay, decay * last + fresh_s[tile, rows, :]))
        return after

    shape = (nblk, 128)
    ends = lax.fori_loop(
        0, size, local, [(jnp.ones(shape, F32), jnp.zeros(shape, F32)) for _ in lanes], unroll=4
    )
    for (tile, sub), (prod, last) in zip(lanes, ends):
        prod_s[tile, sub] = prod
        last_s[tile, sub] = last

    def link(block, carry):
        own = pl.ds(slot_ref[block], 1)
        after = []
        for tile in tiles:
            state = carry[tile]
            for sub in range(SUB):
                carry_s[tile, sub, own, :] = state
                state = prod_s[tile, sub, own, :] * state + last_s[tile, sub, own, :]
            after.append(state)
        return after

    lax.fori_loop(0, nblk, link, [jnp.zeros((1, 128), F32) for _ in tiles])

    def scan(pos, states):
        after = []
        for (tile, sub), state in zip(lanes, states):
            rows = pl.ds(sub * size + pos, nblk, stride=blk + GAP)
            prior_ref[tile, rows, :] = state
            state = decay_s[tile, rows, :] * state + fresh_s[tile, rows, :]
            state_ref[tile, rows, :] = state
            after.append(state)
        return after

    lax.fori_loop(0, size, scan, [carry_s[tile, sub] for tile, sub in lanes], unroll=4)
    ones = jnp.ones((8, 128), F32)

    def gate(slot, _):
        block = nat_ref[slot]
        row = pl.multiple_of(slot * blk, blk)
        out = pl.ds(pl.multiple_of(block * blk, blk), blk)
        held = pl.ds(pl.multiple_of(slot * (blk + GAP), 8), blk)
        square = jnp.zeros((blk, 128), F32)
        for tile in tiles:
            lo = tile * 128
            state = state_ref[tile, held, :]
            pre_g = pre_ref[pl.ds(row, blk), 2 * chans + lo : 2 * chans + lo + 128]
            gated = state * gain_ref[:, lo : lo + 128] * jax.nn.silu(pre_g)
            gated_ref[out, lo : lo + 128] = gated.astype(BF16)
            square += state * state
        sums = lax.dot_general(
            ones,
            square,
            (((1,), (1,)), ((), ())),
            precision=lax.Precision.HIGHEST,
            preferred_element_type=F32,
        )
        square_s[pl.ds(block, 1), :] = sums[:1]
        return 0

    lax.fori_loop(0, nblk, gate, 0)
    high, low = two_terms(square_s[...])
    gated_ref[total:, :128] = jnp.concatenate([high, low], axis=0)
    if chans > 128:
        gated_ref[total:, 128:] = jnp.zeros((2 * nblk, chans - 128), BF16)


def recur_forward(nat, slot, pre, keep, bound, gain, blk):
    chans = bound.shape[1]
    total = keep.shape[0]
    nblk = total // blk
    tiles = chans // 128
    out = jax.ShapeDtypeStruct
    return pl.pallas_call(
        functools.partial(forward_kernel, blk=blk),
        out_shape=(
            out((tiles, nblk * (blk + GAP), 128), F32),
            out((tiles, nblk * (blk + GAP), 128), F32),
            out((total + 2 * nblk, chans), BF16),
        ),
        in_specs=[smem(), smem()] + [vmem()] * 4,
        out_specs=(vmem(),) * 3,
        scratch_shapes=[
            pltpu.VMEM((tiles, nblk * (blk + GAP), 128), F32),
            pltpu.VMEM((tiles, nblk * (blk + GAP), 128), F32),
            pltpu.VMEM((nblk, 128), F32),
            pltpu.VMEM((tiles, SUB, nblk, 128), F32),
            pltpu.VMEM((tiles, SUB, nblk, 128), F32),
            pltpu.VMEM((tiles, SUB, nblk, 128), F32),
        ],
        compiler_params=params(
            [((total, 3 * chans), 4), ((total, 1), 4), ((total + 2 * nblk, chans), 2)]
            + [((tiles, nblk * (blk + GAP), 128), 4)] * 4
        ),
        cost_estimate=cost(total * chans * 30, total * chans * 24, total * chans * 6),
        name="recur_forward",
    )(nat, slot, keep, bound, gain, pre)


def backward_kernel(
    nat_ref, slot_ref, state_ref, prior_ref, keep_ref, bound_ref, gain_ref,
    grad_ref, pre_ref, ext_ref, inv_ref, gpre_ref, gated_ref, gain_sum_ref, bound_sum_ref,
    decay_s, grad_s, prod_s, last_s, carry_s,
    *, blk, width,
):
    chans = bound_ref.shape[1]
    total = gated_ref.shape[0]
    nblk = total // blk
    tiles = range(chans // 128)
    zero_row = jnp.zeros((1, 128), F32)

    def enter(slot, summed):
        at = pl.multiple_of(nat_ref[slot] * blk, blk)
        here = pl.ds(pl.multiple_of(slot * blk, blk), blk)
        held = pl.ds(pl.multiple_of(slot * (blk + GAP), 8), blk)
        ext = ext_ref[here, :].astype(F32)
        inner = (ext[:, 0:1] + ext[:, 1:2]) * (1.0 / width)
        inv = inv_ref[here, 0:1]
        keep = keep_ref[pl.ds(at, blk), :]
        after = []
        for tile in tiles:
            lo = tile * 128
            bound = bound_ref[:, lo : lo + 128]
            gain = gain_ref[:, lo : lo + 128]
            grad = grad_ref[here, lo : lo + 128]
            pre_f = pre_ref[here, chans + lo : chans + lo + 128]
            pre_g = pre_ref[here, 2 * chans + lo : 2 * chans + lo + 128]
            unit = state_ref[tile, held, :] * inv
            sig_g = jax.nn.sigmoid(pre_g)
            act_g = pre_g * sig_g
            scaled = gain * act_g
            grad_s[tile, held, :] = inv * (grad * scaled - unit * inner)
            gated_ref[here, lo : lo + 128] = (unit * scaled).astype(BF16)
            both = grad * unit
            slope = sig_g * (1.0 + pre_g * (1.0 - sig_g))
            gpre_ref[here, 2 * chans + lo : 2 * chans + lo + 128] = (both * gain * slope).astype(
                BF16
            )
            forget = bound + (1.0 - bound) * jax.nn.sigmoid(pre_f)
            decay_s[tile, held, :] = forget * keep
            after.append(summed[tile] + jnp.sum(both * act_g, axis=0, keepdims=True))
        return after

    sums = lax.fori_loop(0, nblk, enter, [zero_row for _ in tiles])
    for tile in tiles:
        gain_sum_ref[:, tile * 128 : tile * 128 + 128] = sums[tile]

    size = blk // SUB
    lanes = [(tile, sub) for tile in tiles for sub in range(SUB)]

    def local(step, carried):
        after = []
        for (tile, sub), (prod, last) in zip(lanes, carried):
            rows = pl.ds((sub + 1) * size - 1 - step, nblk, stride=blk + GAP)
            decay = decay_s[tile, rows, :]
            after.append((prod * decay, decay * (grad_s[tile, rows, :] + last)))
        return after

    shape = (nblk, 128)
    ends = lax.fori_loop(
        0, size, local, [(jnp.ones(shape, F32), jnp.zeros(shape, F32)) for _ in lanes], unroll=4
    )
    for (tile, sub), (prod, last) in zip(lanes, ends):
        prod_s[tile, sub] = prod
        last_s[tile, sub] = last

    def link(step, carry):
        own = pl.ds(slot_ref[nblk - 1 - step], 1)
        after = []
        for tile in tiles:
            back = carry[tile]
            for sub in range(SUB - 1, -1, -1):
                carry_s[tile, sub, own, :] = back
                back = prod_s[tile, sub, own, :] * back + last_s[tile, sub, own, :]
            after.append(back)
        return after

    lax.fori_loop(0, nblk, link, [zero_row for _ in tiles])

    def scan(step, carried):
        after = []
        for (tile, sub), back in zip(lanes, carried):
            rows = pl.ds((sub + 1) * size - 1 - step, nblk, stride=blk + GAP)
            grad = grad_s[tile, rows, :] + back
            grad_s[tile, rows, :] = grad
            after.append(decay_s[tile, rows, :] * grad)
        return after

    lax.fori_loop(0, size, scan, [carry_s[tile, sub] for tile, sub in lanes], unroll=4)

    def leave(slot, summed):
        at = pl.multiple_of(nat_ref[slot] * blk, blk)
        here = pl.ds(pl.multiple_of(slot * blk, blk), blk)
        held = pl.ds(pl.multiple_of(slot * (blk + GAP), 8), blk)
        keep = keep_ref[pl.ds(at, blk), :]
        after = []
        for tile in tiles:
            lo = tile * 128
            bound = bound_ref[:, lo : lo + 128]
            pre_i = pre_ref[here, lo : lo + 128]
            pre_f = pre_ref[here, chans + lo : chans + lo + 128]
            grad = grad_s[tile, held, :]
            sig_i = jax.nn.sigmoid(pre_i)
            sig_f = jax.nn.sigmoid(pre_f)
            forget = bound + (1.0 - bound) * sig_f
            rest = 1.0 - sig_f
            grad_forget = grad * keep * prior_ref[tile, held, :] - grad * (pre_i * sig_i)
            grad_i = grad * (1.0 - forget) * (sig_i * (1.0 + pre_i * (1.0 - sig_i)))
            gpre_ref[here, lo : lo + 128] = grad_i.astype(BF16)
            grad_f = grad_forget * (1.0 - bound) * sig_f * rest
            gpre_ref[here, chans + lo : chans + lo + 128] = grad_f.astype(BF16)
            after.append(summed[tile] + jnp.sum(grad_forget * rest, axis=0, keepdims=True))
        return after

    sums = lax.fori_loop(0, nblk, leave, [zero_row for _ in tiles])
    for tile in tiles:
        bound_sum_ref[:, tile * 128 : tile * 128 + 128] = sums[tile]


def recur_backward(
    nat, slot, grad, pre, ext, inv, state, prior, keep, bound, gain, blk, width
):
    tiles = state.shape[0]
    total = keep.shape[0]
    chans = tiles * 128
    nblk = total // blk
    out = jax.ShapeDtypeStruct
    return pl.pallas_call(
        functools.partial(backward_kernel, blk=blk, width=width),
        out_shape=(
            out((total, 3 * chans), BF16),
            out((total, chans), BF16),
            out((1, chans), F32),
            out((1, chans), F32),
        ),
        in_specs=[smem(), smem()] + [vmem()] * 9,
        out_specs=(vmem(),) * 4,
        scratch_shapes=[
            pltpu.VMEM((tiles, nblk * (blk + GAP), 128), F32),
            pltpu.VMEM((tiles, nblk * (blk + GAP), 128), F32),
            pltpu.VMEM((tiles, SUB, nblk, 128), F32),
            pltpu.VMEM((tiles, SUB, nblk, 128), F32),
            pltpu.VMEM((tiles, SUB, nblk, 128), F32),
        ],
        compiler_params=params(
            [((total, 4 * chans), 4), ((total, 1), 4), ((total, EXT), 4), ((total, EXT), 2)]
            + [((tiles, nblk * (blk + GAP), 128), 4)] * 4
            + [((total, 4 * chans), 2), ((128, width), 4)]
        ),
        cost_estimate=cost(total * chans * 60, total * chans * 36, total * chans * 8),
        name="recur_backward",
    )(nat, slot, state, prior, keep, bound, gain, grad, pre, ext, inv)


def pin(*arrays):
    return [pltpu.with_memory_space_constraint(array, pltpu.HBM) for array in arrays]


def anywhere():
    return pl.BlockSpec(memory_space=pl.ANY)


def part_of(rows, cols, first):
    return pl.BlockSpec((pl.Element(rows), pl.Element(cols)), lambda i: (first, 0))


def pre_kernel(gain_ref, *refs, count):
    blocks, weights = refs[:count], refs[count : count + 3]
    rows_ref, normed_ref, pre_ref, out_w_ref = refs[-4:]
    blk = rows_ref.shape[0] // count
    more = blocks[0].shape[0] - blk
    chans = weights[0].shape[1]
    gain = gain_ref[...]
    for b, block in enumerate(blocks):

        def chunk(step, _, block=block, b=b):
            at = pl.multiple_of(step * 16, 16)
            value = block[pl.ds(at, 16), :]
            out = pl.ds(pl.multiple_of(b * blk + at, 16), 16)
            rows_ref[out, :] = value
            rows = value.astype(F32)
            normed_ref[out, :] = (rows * inverse_rms(rows) * gain).astype(BF16)
            return 0

        lax.fori_loop(0, blk // 16, chunk, 0, unroll=4)
        out_w_ref[b * more : (b + 1) * more, :] = block[blk:, :]
    for k, weight in enumerate(weights):
        pre_ref[:, k * chans : (k + 1) * chans] = dot_nn(normed_ref[...], weight[...])


def make_pre(gain, blocks, weights, held, blk, lo, size, out_lo, out_size):
    both, width = blocks[0].shape
    count = len(blocks)
    rows, more = blk * count, both - blk
    chans = weights[0].shape[1]
    out = jax.ShapeDtypeStruct
    inputs = 4 + count
    there = [k for k, array in enumerate(held) if array is not None]
    return pl.pallas_call(
        functools.partial(pre_kernel, count=count),
        grid=(1,),
        out_shape=(
            pltpu.HBM((size * blk, width), BF16),
            pltpu.HBM((size * blk, width), BF16),
            pltpu.HBM((size * blk, 3 * chans), F32),
            pltpu.HBM((out_size * more, width), BF16),
        ),
        in_specs=[vmem()] * inputs + [anywhere()] * len(there),
        out_specs=(
            part_of(rows, width, lo * blk),
            part_of(rows, width, lo * blk),
            part_of(rows, 3 * chans, lo * blk),
            part_of(more * count, width, (lo - out_lo) * more),
        ),
        input_output_aliases={inputs + n: k for n, k in enumerate(there)},
        compiler_params=params([((rows, width), 2)] * 6 + [((width + 4 * rows, 3 * chans), 2)]),
        cost_estimate=cost(6 * rows * width * chans, rows * width * 6 + 6 * width * chans),
        name="make_pre",
    )(gain, *blocks, *weights, *pin(*(held[k] for k in there)))


def back_kernel(weight_ref, *refs, count):
    blocks, (rows_ref, out_ref) = refs[:count], refs[-2:]
    blk = blocks[0].shape[0]
    for b, block in enumerate(blocks):
        rows_ref[b * blk : (b + 1) * blk, :] = block[...]
    out_ref[...] = dot_nt(rows_ref[...], weight_ref[...])


def make_back(weight, blocks, held, first, total):
    blk, width = blocks[0].shape
    rows, units = blk * len(blocks), weight.shape[0]
    out = jax.ShapeDtypeStruct
    count = 1 + len(blocks)
    return pl.pallas_call(
        functools.partial(back_kernel, count=len(blocks)),
        grid=(1,),
        out_shape=(pltpu.HBM((total, width), BF16), pltpu.HBM((total, units), F32)),
        in_specs=[vmem()] * count + [anywhere()] * len(held),
        out_specs=(part_of(rows, width, first), part_of(rows, units, first)),
        input_output_aliases={count + k: k for k in range(len(held))},
        compiler_params=params([((2 * rows + units, width), 2), ((rows, units), 4)] * 2),
        cost_estimate=cost(2 * rows * width * units, (rows + units) * width * 2),
        name="make_back",
    )(weight, *blocks, *pin(*held))


def gated_grad_kernel(weight_ref, *refs, count):
    blocks, (rows_ref, out_ref, ext_ref) = refs[:count], refs[-3:]
    blk = blocks[0].shape[0]
    width = rows_ref.shape[1]
    for b, block in enumerate(blocks):
        rows_ref[b * blk : (b + 1) * blk, :] = block[:, :width]
        ext_ref[b * blk : (b + 1) * blk, :] = block[:, width:]
    out_ref[...] = dot_nt(rows_ref[...], weight_ref[...])


def make_gated_grad(weight, blocks, held, first, total):
    chans, width = weight.shape
    blk = blocks[0].shape[0]
    rows = blk * len(blocks)
    out = jax.ShapeDtypeStruct
    count = 1 + len(blocks)
    return pl.pallas_call(
        functools.partial(gated_grad_kernel, count=len(blocks)),
        grid=(1,),
        out_shape=(pltpu.HBM((total, width), BF16), pltpu.HBM((total, chans), F32), pltpu.HBM((total, EXT), BF16)),
        in_specs=[vmem()] * count + [anywhere()] * len(held),
        out_specs=(
            part_of(rows, width, first),
            part_of(rows, chans, first),
            part_of(rows, EXT, first),
        ),
        input_output_aliases={count + k: k for k in range(len(held))},
        compiler_params=params([((2 * rows + chans, width + EXT), 2), ((rows, chans), 4)] * 2),
        cost_estimate=cost(2 * rows * width * chans, (rows + chans) * width * 2),
        name="make_gated_grad",
    )(weight, *blocks, *pin(*held))


def mix_kernel(at_ref, nat_ref, w_a, w_b, w_c, w_d, *refs, count, held):
    gated, (out_ref, weight_s, gated_s) = refs[:count], refs[-3:]
    chans = gated[0].shape[1]
    rows = chans // 4

    @pl.when(pl.program_id(0) == 0)
    def _():
        for k in range(count):
            for part, weight in enumerate((w_a, w_b, w_c, w_d)):
                to = pl.multiple_of(k * chans + at_ref[part] * rows, rows)
                weight_s[pl.ds(to, rows), :] = weight[k * rows : (k + 1) * rows, :]

    for k in range(count):
        gated_s[:, k * chans : (k + 1) * chans] = gated[k][...]
    tile = 512
    for col in range(0, out_ref.shape[1], tile):
        summed = dot_nn(gated_s[...], weight_s[:, col : col + tile])
        if held:
            summed += refs[count][:, col : col + tile]
        out_ref[:, col : col + tile] = summed


def make_mix(nat, at, gated, weights, held, blk):
    count = len(gated)
    chans = gated[0].shape[1]
    width = weights[0].shape[1]
    nblk = nat.shape[0]
    whole = pl.BlockSpec(weights[0].shape, lambda i, at, nat: (0, 0), pipeline_mode=pl.Buffered(1))
    rows = pl.BlockSpec((blk, width), lambda i, at, nat: (i, 0))
    more = [] if held is None else [held]
    return pl.pallas_call(
        functools.partial(mix_kernel, count=count, held=bool(more)),
        out_shape=pltpu.HBM((nblk * blk, width), F32),
        grid_spec=pltpu.PrefetchScalarGridSpec(
            num_scalar_prefetch=2,
            grid=(nblk,),
            in_specs=[whole] * 4
            + [pl.BlockSpec((blk, chans), lambda i, at, nat: (nat[i], 0))] * count
            + [rows] * len(more),
            out_specs=rows,
            scratch_shapes=[
                pltpu.VMEM((count * chans, width), BF16),
                pltpu.VMEM((blk, count * chans), BF16),
            ],
        ),
        input_output_aliases={6 + count: 0} if more else {},
        compiler_params=params(
            [(weights[0].shape, 2)] * 4
            + [((count * chans, width), 2), ((blk, count * chans), 2)]
            + [((blk, chans), 2)] * (2 * count)
            + [((blk, width), 4)] * 5
        ),
        cost_estimate=cost(
            2 * nblk * blk * count * chans * width,
            count * chans * width * 2 + nblk * blk * (width * 4 + count * chans * 2),
        ),
        name="make_mix",
    )(at, nat, *weights, *gated, *pin(*more))


def glu_kernel(
    nat_ref, at_ref, gated_ref, w_a, w_b, w_c, w_d, mixed_ref, rows_ref, square_ref, gain_ref,
    gate_w_ref, up_w_ref, back_ref, *refs, first, count,
):
    normed_ref, hidden_ref, grad_gate_ref, grad_up_ref, inv_ref, term_ref, *own = refs[count:]
    step = pl.program_id(0)
    blk, width = rows_ref.shape
    *own, weight_s = own

    @pl.when(step == 0)
    def _():
        for part, weight in enumerate((w_a, w_b, w_c, w_d)):
            size = weight.shape[0]
            weight_s[pl.ds(pl.multiple_of(at_ref[part] * size, size), size), :] = weight[...]

    square = square_ref[pl.ds(nat_ref[first + step], 1), :]
    row = lax.broadcasted_iota(jnp.int32, (blk, blk), 0)
    col = lax.broadcasted_iota(jnp.int32, (blk, blk), 1)
    square = jnp.sum(jnp.where(row == col, square, 0.0), axis=1, keepdims=True)
    inv = lax.rsqrt(square / width + EPS)
    mixed = mixed_ref[...] + dot_nn(gated_ref[...], weight_s[...])
    middle = rows_ref[...].astype(F32) + mixed * inv
    inv_two = inverse_rms(middle)
    normed_ref[...] = (middle * inv_two * gain_ref[...]).astype(BF16)
    lane = lax.broadcasted_iota(jnp.int32, (blk, EXT), 1)
    inv_ref[...] = jnp.where(lane == 0, inv, jnp.where(lane == 1, inv_two, 0.0))
    if own:

        @pl.when(step == 0)
        def _():
            own[0][...] = middle

    gate = dot_nt(normed_ref[...], gate_w_ref[...])
    up = dot_nt(normed_ref[...], up_w_ref[...])
    back = back_ref[...]
    sig = jax.nn.sigmoid(gate)
    act = gate * sig
    hidden_ref[...] = (act * up).astype(BF16)
    grad_gate_ref[...] = (back * up * (sig * (1.0 + gate * (1.0 - sig)))).astype(BF16)
    grad_up_ref[...] = (back * act).astype(BF16)
    term_ref[...] = (
        dot_nn(grad_gate_ref[...], gate_w_ref[...]) + dot_nn(grad_up_ref[...], up_w_ref[...])
    ).astype(BF16)


def make_glu(nat, at, gated, weights, mixed, rows, square, gain, gate_w, up_w, back, held, lo, hi):
    total, width = rows.shape
    blk = square.shape[1]
    chans, units = gated.shape[1], gate_w.shape[0]
    out = jax.ShapeDtypeStruct

    def fixed(value):
        return pl.BlockSpec(
            value.shape, lambda i, nat, at: (0,) * value.ndim, pipeline_mode=pl.Buffered(1)
        )

    def tiled(cols, base=lo):
        return pl.BlockSpec((blk, cols), lambda i, nat, at: (base + i, 0))

    shapes = [pltpu.HBM((total, width), BF16)] + [pltpu.HBM((total, units), BF16)] * 3
    shapes += [pltpu.HBM((total, EXT), F32), out(((hi - lo) * blk, width), BF16)]
    specs = [tiled(width)] + [tiled(units)] * 3 + [tiled(EXT), tiled(width, 0)]
    if lo == 0:
        shapes.append(out((blk, width), F32))
        specs.append(pl.BlockSpec((blk, width), lambda i, nat, at: (0, 0)))
    return pl.pallas_call(
        functools.partial(glu_kernel, first=lo, count=len(held)),
        out_shape=shapes,
        grid_spec=pltpu.PrefetchScalarGridSpec(
            num_scalar_prefetch=2,
            grid=(hi - lo,),
            in_specs=[pl.BlockSpec((blk, chans), lambda i, nat, at: (nat[lo + i], 0))]
            + [pl.BlockSpec((chans // 4, width), lambda i, nat, at: (2, 0))] * 4
            + [tiled(width), tiled(width), fixed(square), fixed(gain)]
            + [fixed(gate_w), fixed(up_w), tiled(units)]
            + [anywhere()] * len(held),
            out_specs=specs,
            scratch_shapes=[pltpu.VMEM((chans, width), BF16)],
        ),
        input_output_aliases={14 + k: k for k in range(len(held))},
        compiler_params=params(
            [((chans, width), 2)] * 3
            + [(gate_w.shape, 2)] * 2
            + [((blk, width), 4)] * 12
            + [((blk, units), 4)] * 10
        ),
        cost_estimate=cost(
            (hi - lo) * blk * width * (2 * chans + 8 * units),
            (hi - lo) * blk * width * 8 + 4 * units * width,
        ),
        name="make_glu",
    )(nat, at, *pin(gated, *weights, mixed, rows), square, gain, *pin(gate_w, up_w, back, *held))


def matmul_kernel(lhs_ref, rhs_ref, out_ref):
    out_ref[...] = dot_nn(lhs_ref[...], rhs_ref[...]).astype(out_ref.dtype)


def make_product(lhs, rhs, blk, lo, hi):
    inner, width = rhs.shape
    rows = (hi - lo) * blk
    return pl.pallas_call(
        matmul_kernel,
        grid=(hi - lo,),
        out_shape=jax.ShapeDtypeStruct((rows, width), BF16),
        in_specs=[
            pl.BlockSpec((blk, inner), lambda i: (lo + i, 0)),
            pl.BlockSpec((inner, width), lambda i: (0, 0), pipeline_mode=pl.Buffered(1)),
        ],
        out_specs=pl.BlockSpec((blk, width), lambda i: (i, 0)),
        compiler_params=params([((inner, width), 2)] + [((blk, width + inner), 4)] * 5),
        cost_estimate=cost(2 * rows * inner * width, (rows * inner + (rows + inner) * width) * 2),
        name="make_product",
    )(lhs, rhs)


def last_kernel(gpre_ref, w_a, w_b, w_c, normed_ref, term_ref, sum_ref):
    chans = w_a.shape[1]
    total = None
    for k, weight in enumerate((w_a, w_b, w_c)):
        term = dot_nt(gpre_ref[:, k * chans : (k + 1) * chans], weight[...])
        total = term if total is None else total + term
    term_ref[...] = total.astype(BF16)
    part = jnp.sum(total * normed_ref[...].astype(F32), axis=0, keepdims=True)

    @pl.when(pl.program_id(0) == 0)
    def _():
        sum_ref[...] = jnp.zeros_like(sum_ref)

    sum_ref[...] += part


def make_last(gpre, weights, normed, blk, lo, hi):
    width, chans = weights[0].shape
    rows = (hi - lo) * blk
    out = jax.ShapeDtypeStruct
    fixed = pl.BlockSpec((width, chans), lambda i: (0, 0), pipeline_mode=pl.Buffered(1))
    return pl.pallas_call(
        last_kernel,
        grid=(hi - lo,),
        out_shape=(out((rows, width), BF16), out((1, width), F32)),
        in_specs=[pl.BlockSpec((blk, 3 * chans), lambda i: (lo + i, 0))]
        + [fixed] * 3
        + [pl.BlockSpec((blk, width), lambda i: (lo + i, 0))],
        out_specs=(
            pl.BlockSpec((blk, width), lambda i: (i, 0)),
            pl.BlockSpec((1, width), lambda i: (0, 0)),
        ),
        compiler_params=params([((width, chans), 2)] * 3 + [((blk, width), 4)] * 8),
        cost_estimate=cost(6 * rows * width * chans, rows * width * 4 + 6 * width * chans),
        name="make_last",
    )(gpre, *weights, normed)


def middle_grad_kernel(
    r_ref, l_ref, part_ref, rows_ref, middle_ref, inv_ref, cot_ref, weight_ref, gain_ref,
    grad_ref, send_ref, gain_sum_ref,
):
    blk, width = rows_ref.shape
    gain = gain_ref[...]
    weight = weight_ref[0, 0]

    def chunk(step, summed):
        rows = pl.ds(pl.multiple_of(step * 16, 16), 16)
        grad_two = (
            r_ref[rows, :].astype(F32) + l_ref[rows, :].astype(F32) + part_ref[rows, :].astype(F32)
        )
        inv_two = inv_ref[rows, 1:2]
        middle = middle_ref[rows, :]
        unit = middle * inv_two
        scaled = grad_two * gain
        mean = jnp.mean(scaled * unit, axis=1, keepdims=True)
        grad = cot_ref[rows, :].astype(F32) * weight + inv_two * (scaled - unit * mean)
        grad_ref[rows, :] = grad
        sent = grad.astype(BF16)
        send_ref[rows, :width] = sent
        mix = middle - rows_ref[rows, :].astype(F32)
        inner = jnp.sum(sent.astype(F32) * mix, axis=1, keepdims=True)
        high, low = two_terms(inner)
        lane = lax.broadcasted_iota(jnp.int32, (16, EXT), 1)
        ext = jnp.where(
            lane == 0, high.astype(F32), jnp.where(lane == 1, low.astype(F32), 0.0)
        )
        send_ref[rows, width:] = ext.astype(BF16)
        return summed + jnp.sum(grad_two * unit, axis=0, keepdims=True)

    gain_sum_ref[...] = lax.fori_loop(0, blk // 16, chunk, jnp.zeros((1, width), F32))


def make_middle_grad(r_in, l_in, part, rows, middle, inv, cot, weight, gain):
    blk, width = rows.shape
    out = jax.ShapeDtypeStruct
    return pl.pallas_call(
        middle_grad_kernel,
        grid=(1,),
        out_shape=(
            out((blk, width), F32),
            out((blk, width + EXT), BF16),
            out((1, width), F32),
        ),
        in_specs=[vmem(), vmem(), pl.BlockSpec((blk, width), lambda i: (0, 0))]
        + [vmem()] * 2
        + [pl.BlockSpec((blk, EXT), lambda i: (0, 0)), vmem()]
        + [smem(), vmem()],
        out_specs=(vmem(),) * 3,
        compiler_params=params([((blk, width + EXT), 4)] * 6),
        cost_estimate=cost(blk * width * 16, blk * width * 20),
        name="make_middle_grad",
    )(r_in, l_in, part, rows, middle, inv, cot, weight, gain)


def final_kernel(
    r_ref, l_ref, part_ref, rows_ref, grad_ref, gain_ref, out_ref,
):
    blk = rows_ref.shape[0]
    gain = gain_ref[...]

    def chunk(step, _):
        at = pl.multiple_of(step * 16, 16)
        rows = pl.ds(at, 16)
        grad = (
            r_ref[rows, :].astype(F32) + l_ref[rows, :].astype(F32) + part_ref[rows, :].astype(F32)
        )
        own = rows_ref[rows, :].astype(F32)
        inv = inverse_rms(own)
        unit = own * inv
        scaled = grad * gain
        mean = jnp.mean(scaled * unit, axis=1, keepdims=True)
        out_ref[rows, :] = grad_ref[rows, :] + inv * (scaled - unit * mean)
        return 0

    lax.fori_loop(0, blk // 16, chunk, 0)


def make_final(r_in, l_in, part, rows, grad, gain):
    blk, width = rows.shape
    return pl.pallas_call(
        final_kernel,
        out_shape=jax.ShapeDtypeStruct((blk, width), F32),
        in_specs=[vmem()] * 6,
        out_specs=vmem(),
        compiler_params=params([((blk, width), 4)] * 8),
        cost_estimate=cost(blk * width * 16, blk * width * 18),
        name="make_final",
    )(r_in, l_in, part, rows, grad, gain)


class Ring:
    def __init__(self, size):
        self.size = size
        self.steps = size // 2
        order = list(range(0, size, 2)) + list(range(size - 1, 0, -2))
        place = {device: at for at, device in enumerate(order)}
        self.right = [(order[i], order[(i + 1) % size]) for i in range(size)]
        self.left = [(b, a) for a, b in self.right]
        offs = [0]
        for k in range(1, self.steps):
            offs += [-k, k]
        offs.append(self.steps)
        cuts = [0, *range(3, size, 2), size]
        self.spans = list(zip(cuts[:-1], cuts[1:]))
        self.pairs = [(0, 1), (1, 3), *self.spans[1:]]
        nat = np.zeros((size, size), np.int32)
        slot = np.zeros((size, size), np.int32)
        for device in range(size):
            for at, off in enumerate(offs):
                block = order[(place[device] + off) % size]
                nat[device, at] = block
                slot[device, block] = at
        self.nat, self.slot = nat, slot

    def move(self, right, left):
        return lax.ppermute(right, "mp", self.right), lax.ppermute(left, "mp", self.left)

    def gather(self, k, pair):
        right, left = pair
        if k == self.steps - 1:
            rows = right.shape[0] // 32 * 16
            return self.move(right[:rows], left[rows:])
        return self.move(right, left)

    def scatter(self, k, pair, group):
        if k == 0:
            rows = group.shape[0] // 2
            return self.move(group[:rows], group[rows:])
        right, left = pair
        blk = group.shape[0] // 2
        to_left, to_right = group[:blk], group[blk:]
        if k == 1:
            rows = blk // 2
            right = jnp.concatenate([add(right, to_right[:rows]), to_right[rows:]], axis=0)
            left = jnp.concatenate([to_left[:rows], add(left, to_left[rows:])], axis=0)
        else:
            right, left = add(right, to_right), add(left, to_left)
        return self.move(right, left)


def close(*values):
    return lax.optimization_barrier(values)


def add(a, b):
    return (a.astype(F32) + b.astype(F32)).astype(BF16)


def dp_swap(value, bit):
    return lax.ppermute(value, "dp", [(i, i ^ bit) for i in range(lax.axis_size("dp"))])


def mp_swap(value, bit):
    return lax.ppermute(value, "mp", [(i, i ^ bit) for i in range(lax.axis_size("mp"))])


def local(
    block_input,
    out_cotangent,
    segments,
    domain_tags,
    counts,
    attn_gain,
    mlp_gain,
    norm_gain,
    bound_table,
    w_input,
    w_forget,
    w_gate_mix,
    w_out,
    w_glu_gate,
    w_glu_up,
    w_glu_down,
):
    blk, width = block_input.shape
    chans = w_input.shape[1]
    seqs = segments.shape[0]
    total = seqs * LEN
    mp_size, dp_size = lax.axis_size("mp"), lax.axis_size("dp")
    mp_index, dp_index = lax.axis_index("mp"), lax.axis_index("dp")
    ring = Ring(mp_size)
    spans, steps = ring.spans, ring.steps
    last = steps - 1
    nat = lax.dynamic_index_in_dim(jnp.asarray(ring.nat), mp_index, 0, keepdims=False)
    slot = lax.dynamic_index_in_dim(jnp.asarray(ring.slot), mp_index, 0, keepdims=False)
    at = dp_index ^ jnp.array([0, 2, 1, 3], jnp.int32)

    lanes = -(-chans // 128) * 128
    pad = lanes - chans

    def pad_cols(array):
        return jnp.pad(array, ((0, 0), (0, pad))) if pad else array

    mix_weights = [pad_cols(w_input), pad_cols(w_forget), pad_cols(w_gate_mix)]
    w_out_pad = jnp.pad(w_out, ((0, pad), (0, 0))) if pad else w_out
    attn_row, mlp_row = attn_gain[None, :], mlp_gain[None, :]
    gate_w, up_w = w_glu_gate.T, w_glu_up.T

    layer_ids = jnp.arange(NLAYER)
    pick = ((layer_ids >= 1) & (layer_ids <= LAYER)).astype(F32)[:, None]
    bound = pad_cols(jnp.sum(jax.nn.softmax(bound_table, axis=0) * pick, axis=0)[None, :])
    gain = pad_cols(norm_gain[None, :])
    keep = jnp.concatenate(
        [jnp.zeros((seqs, 1), F32), (segments[:, 1:] == segments[:, :-1]).astype(F32)], axis=1
    ).reshape(total, 1)
    seq_count = jnp.sum(
        jnp.where(
            domain_tags[:, None] == jnp.arange(NDOM)[None, :], counts.astype(F32)[None, :], 0.0
        ),
        axis=1,
    )
    weight = lax.dynamic_slice_in_dim(lax.rsqrt(seq_count), mp_index * blk // LEN, 1, 0)
    grad_b = (out_cotangent.astype(F32) * weight[:, None]).astype(BF16)


    quarter = lax.dynamic_slice_in_dim(w_out_pad, dp_index * (lanes // 4), lanes // 4, axis=0)
    own = jnp.concatenate([block_input, quarter], axis=0)
    pair, waiting, held = (own, own), [own], (None,) * 4
    table = bound_table[None]
    split = spans[last - 1][0]

    def pre_group(blocks, held, g):
        part = (split, mp_size - split) if spans[g][0] >= split else (0, split)
        return make_pre(attn_row, blocks, mix_weights, held, blk, spans[g][0], mp_size, *part)

    for k in range(steps):
        pair = ring.gather(k, pair)
        if k == 0:
            more = mp_swap(table, 1)
            pair, bound, keep, grad_b = close(pair, bound, keep, grad_b)
            waiting += pair
            continue
        held = pre_group(waiting, held, k - 1)
        if k == 1:
            pair, held, more = close(pair, held, more)
            table = jnp.concatenate([table, more], axis=0)
        elif k < last:
            if k == last - 1:
                *held, out_own = held
                near = [out_own, dp_swap(out_own, 2), dp_swap(out_own, 1)]
                more = mp_swap(table, 2)
                pair, held, near[2], grad_b = close(pair, held, near[2], grad_b)
                held = (*held, None)
            else:
                pair, held = close(pair, held)
        else:
            cot = ring.gather(0, (grad_b, grad_b))
            pair, held, more, near[1] = close(pair, held, more, near[1])
            table = jnp.concatenate([table, more], axis=0)
        waiting = list(pair) if k < last else [jnp.concatenate(pair, axis=0)]
    rows, normed, pre, out_own = pre_group(waiting, held, last)

    near.append(dp_swap(near[1], 1))
    far = [out_own, dp_swap(out_own, 2), dp_swap(out_own, 1)]
    state, prior, gated_own = recur_forward(nat, slot, pre, keep, bound, gain, blk)
    gated_own, cot = close(gated_own, cot)
    pair, gated_blocks, mixed = (gated_own, gated_own), [gated_own], None
    held, cot_waiting = (), [grad_b]
    reach = 4
    for k in range(steps):
        pair = ring.gather(k, pair)
        if k == 0:
            pair, near, far[2], cot = close(pair, near, far[2], cot)
            cot_waiting += cot
        else:
            cot = ring.gather(k, cot)
            held = make_back(w_glu_down, cot_waiting, held, spans[k - 1][0] * blk, total)
            if k < last:
                if reach < mp_size:
                    more = mp_swap(table, reach)
                    reach *= 2
                else:
                    more = table[:0]
                if k == last - 1:
                    mixed = make_mix(nat, at, gated_blocks, near, None, blk)
                    pair, cot, held, more, mixed, far[1] = close(
                        pair, cot, held, more, mixed, far[1]
                    )
                    far.append(dp_swap(far[1], 1))
                else:
                    pair, cot, held, more = close(pair, cot, held, more)
                table = jnp.concatenate([table, more], axis=0)
            else:
                mixed = make_mix(nat, at, gated_blocks[split:], far, mixed, blk)
                pair, cot, held, mixed = close(pair, cot, held, mixed)
            cot_waiting = list(cot) if k < last else [jnp.concatenate(cot, axis=0)]
        gated_blocks += pair if k < last else [jnp.concatenate(pair, axis=0)]
    cot_all, back = make_back(w_glu_down, cot_waiting, held, spans[last][0] * blk, total)
    squares = sum(block[total:, :128].astype(F32) for block in gated_blocks)
    squares = squares[:mp_size] + squares[mp_size:]

    pairs = ring.pairs

    def glu_group(held, g):
        return make_glu(
            nat, at, gated_blocks[-1], far, mixed, rows, squares, mlp_row, gate_w, up_w,
            back, held, *pairs[g],
        )

    def out_group(g):
        return make_product(hidden, w_glu_down, blk, *pairs[g])

    made = glu_group((), steps)
    held, term = made[:5], made[5]
    for k in range(steps):
        pair = ring.scatter(k, pair, term)
        made = glu_group(held, last - k)
        held, term = made[:5], made[5]
        pair, held, term = close(pair, held, term)
    two, hidden, grad_gate, grad_up, inv = held
    middle = made[6]
    outs = [None] * (steps + 1)
    outs[steps] = out_group(steps)
    grad_middle, sent, mlp_term = make_middle_grad(
        *pair, term, block_input, middle, inv, out_cotangent, weight[:, None], mlp_row
    )

    size = width // dp_size

    def cols(array, bits):
        return lax.dynamic_slice_in_dim(array, (dp_index ^ bits) * size, size, axis=1)

    def far_slice(own, rest):
        return (own[0] + rest[0].astype(F32)).astype(BF16)

    def slice_sum(own, rest, far):
        return own[1] + rest[1].astype(F32) + far.astype(F32)

    def slices(left, right, which, split_left=False):
        found = []
        for bits in ((3, 1) if which == "rest" else (2, 0)):
            if split_left:
                found.append(dot_tn(cols(left, bits), right))
            else:
                found.append(dot_tn(left, cols(right, bits)))
        return jnp.stack([value.astype(BF16) for value in found]) if which == "rest" else found

    sent, hidden, two, cot_all, grad_gate, grad_up = close(
        sent, hidden, two, cot_all, grad_gate, grad_up
    )
    pair, res, sent_waiting, held = (sent, sent), (), [sent], ()
    for k in range(steps):
        pair = ring.gather(k, pair)
        res = ring.scatter(k, res, outs[steps - k])
        outs[last - k] = out_group(last - k)
        if k:
            held = make_gated_grad(w_out_pad, sent_waiting, held, spans[k - 1][0] * blk, total)
        if k == 0:
            down = slices(hidden, cot_all, "rest"), slices(hidden, cot_all, "own")
            pair, res, outs[last], down, two, hidden = close(
                pair, res, outs[last], down, two, hidden
            )
            sent_waiting += pair
            continue
        if k == 1:
            down_rest = dp_swap(down[0], 1)
            gate = slices(grad_gate, two, "rest"), slices(grad_gate, two, "own")
            pair, res, outs, held, down_rest, gate, two, hidden = close(
                pair, res, outs, held, down_rest, gate, two, hidden
            )
        elif k == 2:
            down_far = dp_swap(far_slice(down[1], down_rest), 2)
            gate_rest = dp_swap(gate[0], 1)
            up = slices(grad_up, two, "rest"), slices(grad_up, two, "own")
            pair, res, outs, held, gate_rest, up, hidden = close(
                pair, res, outs, held, gate_rest, up, hidden
            )
        elif k < last:
            pair, res, outs, held = close(pair, res, outs, held)
        if k == last:
            up_rest = dp_swap(up[0], 1)
            pair, held, up_rest, outs[0] = close(pair, held, up_rest, outs[0])
        sent_waiting = list(pair) if k < last else [jnp.concatenate(pair, axis=0)]
    sent_all, grad, ext = make_gated_grad(
        w_out_pad, sent_waiting, held, spans[last][0] * blk, total
    )

    grad_pre, gated, norm_term, bound_grad = recur_backward(
        nat, slot, grad, pre, ext, inv, state, prior, keep, bound, gain, blk, width
    )

    def last_group(g, grad_pre):
        return make_last(grad_pre, mix_weights, normed, blk, *pairs[g])

    def placed(row):
        wide = jnp.zeros((1, width), F32)
        return lax.dynamic_update_slice(wide, row[:, :chans], (0, mp_index * chans))

    lasts = [None] * (steps + 1)
    lasts[steps] = last_group(steps, grad_pre)
    for k in range(steps):
        pair = ring.scatter(k, pair, lasts[steps - k][0])
        if k == 0:
            gate_far = dp_swap(far_slice(gate[1], gate_rest), 2)
            lasts[last] = last_group(last, grad_pre)
            mix_rest = slices(normed, grad_pre, "rest", True)
            pair, res, lasts[last], mix_rest, grad_pre, normed, gated, sent_all, down_far, up = close(
                pair, res, lasts[last], mix_rest, grad_pre, normed, gated, sent_all, down_far, up
            )
        elif k == 1:
            mix_rest = dp_swap(mix_rest, 1)
            up_far = dp_swap(far_slice(up[1], up_rest), 2)
            for g in range(last):
                lasts[g] = last_group(g, grad_pre)
            mix = slices(normed, grad_pre, "own", True)
            down, res, outs[0] = close(down, res, outs[0])
            pair, lasts, mix_rest, mix, gated, sent_all, gate_far, down, res, up = close(
                pair, lasts, mix_rest, mix, gated, sent_all, gate_far, down, res, up
            )
        elif k == 2:
            mix_far = dp_swap(far_slice(mix, mix_rest), 2)
            out = slices(gated, sent_all, "rest"), slices(gated, sent_all, "own")
            down_grad = slice_sum(down[1], down_rest, down_far)
            result = (
                middle + res[0].astype(F32) + res[1].astype(F32) + outs[0].astype(F32)
            ).astype(BF16)

            attn_term = sum(found[1] for found in lasts) / attn_row
            packed = jnp.concatenate(
                [attn_term, mlp_term, placed(norm_term), placed(bound_grad)], axis=0
            ).reshape(-1, 128)
            packed = packed + dp_swap(packed, 1)
            packed = packed + mp_swap(packed, 1)
            pair, out, down_grad, result, packed, gate, up, up_far = close(
                pair, out, down_grad, result, packed, gate, up, up_far
            )
        elif k < last:
            (pair,) = close(pair)
        else:
            out_rest = dp_swap(out[0], 1)
            packed = packed + mp_swap(packed, 2)
            packed = packed + dp_swap(packed, 2)
            glu_gate_grad = slice_sum(gate[1], gate_rest, gate_far)
            glu_up_grad = slice_sum(up[1], up_rest, up_far)
            pair, packed, out_rest, glu_gate_grad, glu_up_grad, mix_far = close(
                pair, packed, out_rest, glu_gate_grad, glu_up_grad, mix_far
            )
    out_far = dp_swap(far_slice(out[1], out_rest), 2)
    reach = 4
    while reach < mp_size:
        packed = packed + mp_swap(packed, reach)
        reach *= 2
    grad_block_input = make_final(*pair, lasts[0][0], block_input, grad_middle, attn_row)
    mix_grad = slice_sum(mix, mix_rest, mix_far)
    out_grad = slice_sum(out[1], out_rest, out_far)[:chans]
    glu_gate_grad, glu_up_grad = glu_gate_grad.T, glu_up_grad.T

    attn_sum, mlp_sum, norm_sum, bound_sum = packed.reshape(4, width)
    table = jnp.take(table, jnp.arange(mp_size) ^ mp_index, axis=0)
    shares = jax.nn.softmax(table.transpose(1, 0, 2).reshape(NLAYER, width), axis=0)
    pick_grad = pick * bound_sum[None, :]
    table_sum = shares * (pick_grad - jnp.sum(shares * pick_grad, axis=0, keepdims=True))
    return (
        result,
        grad_block_input,
        attn_sum,
        mlp_sum,
        norm_sum,
        table_sum,
        mix_grad[:, :chans],
        mix_grad[:, lanes : lanes + chans],
        mix_grad[:, 2 * lanes : 2 * lanes + chans],
        out_grad,
        glu_gate_grad,
        glu_up_grad,
        down_grad,
    )


def solution(mesh):
    placed = (
        P(("dp", "mp"), None),
        P(("dp", "mp"), None),
        P("dp", None),
        P("dp"),
        P(),
        P(),
        P(),
        P("mp"),
        P(None, "mp"),
        P(None, "mp"),
        P(None, "mp"),
        P(None, "mp"),
        P("mp", None),
        P(None, "mp"),
        P(None, "mp"),
        P("mp", None),
    )
    return jax.shard_map(
        local,
        mesh=mesh,
        in_specs=placed,
        out_specs=(
            P(("dp", "mp"), None),
            P(("dp", "mp"), None),
            P(),
            P(),
            P(),
            P(),
            P("dp", "mp"),
            P("dp", "mp"),
            P("dp", "mp"),
            P("mp", "dp"),
            P("dp", "mp"),
            P("dp", "mp"),
            P("mp", "dp"),
        ),
        check_vma=False,
    )
```

```python
import functools

import jax
import jax.numpy as jnp
import numpy as np
from jax import lax
from jax.experimental import pallas as pl
from jax.experimental.pallas import tpu as pltpu
from jax.sharding import PartitionSpec as P

NLAYER = 24
LAYER = 20
LEN = 1024
NDOM = 8
EXT = 128
SUB = 4
GAP = 8
EPS = 1e-06
F32 = jnp.float32
BF16 = jnp.bfloat16
MIB = 1 << 20
GRANT = 0


def vmem():
    return pl.BlockSpec(memory_space=pltpu.VMEM)


def smem():
    return pl.BlockSpec(memory_space=pltpu.SMEM)


def params(arrays, least=GRANT):
    used = 0
    for shape, item in arrays:
        lead = int(np.prod(shape[:-2])) if len(shape) > 2 else 1
        used += lead * (-(-shape[-2] // 16) * 16) * (-(-shape[-1] // 128) * 128) * item
    return pltpu.CompilerParams(vmem_limit_bytes=max(used + used // 8 + 2 * MIB, least * MIB))


def tie(value, *after):
    return lax.optimization_barrier((value, *after))[0]


def cost(flops, nbytes, trans=0, scale=1):
    return pl.CostEstimate(
        flops=scale * flops, bytes_accessed=scale * nbytes, transcendentals=scale * trans
    )


def joined(refs):
    return refs[0][...] if len(refs) == 1 else jnp.concatenate([ref[...] for ref in refs], axis=0)


def dot_tn(lhs, rhs):
    return lax.dot_general(lhs, rhs, (((0,), (0,)), ((), ())), preferred_element_type=F32)


def dot_nt(lhs, rhs):
    return lax.dot_general(lhs, rhs, (((1,), (1,)), ((), ())), preferred_element_type=F32)


def dot_nn(lhs, rhs):
    return jnp.dot(lhs, rhs, preferred_element_type=F32)


def inverse_rms(rows):
    return lax.rsqrt(jnp.mean(rows * rows, axis=1, keepdims=True) + EPS)


def two_terms(value):
    high = value.astype(BF16)
    return high, (value - high.astype(F32)).astype(BF16)


def forward_kernel(
    nat_ref, slot_ref, keep_ref, bound_ref, gain_ref, pre_ref,
    state_ref, prior_ref, gated_ref, decay_s, fresh_s, square_s, prod_s, last_s, carry_s,
    *, blk,
):
    chans = bound_ref.shape[1]
    total = keep_ref.shape[0]
    nblk = total // blk
    tiles = range(chans // 128)

    def gates(slot, _):
        at = pl.multiple_of(nat_ref[slot] * blk, blk)
        row = pl.multiple_of(slot * blk, blk)
        out = pl.ds(pl.multiple_of(slot * (blk + GAP), 8), blk)
        keep = keep_ref[pl.ds(at, blk), :]
        for tile in tiles:
            lo = tile * 128
            bound = bound_ref[:, lo : lo + 128]
            pre_i = pre_ref[pl.ds(row, blk), lo : lo + 128]
            pre_f = pre_ref[pl.ds(row, blk), chans + lo : chans + lo + 128]
            forget = bound + (1.0 - bound) * jax.nn.sigmoid(pre_f)
            decay_s[tile, out, :] = forget * keep
            fresh_s[tile, out, :] = jax.nn.silu(pre_i) * (1.0 - forget)
        return 0

    lax.fori_loop(0, nblk, gates, 0)
    size = blk // SUB
    lanes = [(tile, sub) for tile in tiles for sub in range(SUB)]

    def local(pos, carried):
        after = []
        for (tile, sub), (prod, last) in zip(lanes, carried):
            rows = pl.ds(sub * size + pos, nblk, stride=blk + GAP)
            decay = decay_s[tile, rows, :]
            after.append((prod * decay, decay * last + fresh_s[tile, rows, :]))
        return after

    shape = (nblk, 128)
    ends = lax.fori_loop(
        0, size, local, [(jnp.ones(shape, F32), jnp.zeros(shape, F32)) for _ in lanes], unroll=4
    )
    for (tile, sub), (prod, last) in zip(lanes, ends):
        prod_s[tile, sub] = prod
        last_s[tile, sub] = last

    def link(block, carry):
        own = pl.ds(slot_ref[block], 1)
        after = []
        for tile in tiles:
            state = carry[tile]
            for sub in range(SUB):
                carry_s[tile, sub, own, :] = state
                state = prod_s[tile, sub, own, :] * state + last_s[tile, sub, own, :]
            after.append(state)
        return after

    lax.fori_loop(0, nblk, link, [jnp.zeros((1, 128), F32) for _ in tiles])

    def scan(pos, states):
        after = []
        for (tile, sub), state in zip(lanes, states):
            rows = pl.ds(sub * size + pos, nblk, stride=blk + GAP)
            prior_ref[tile, rows, :] = state
            state = decay_s[tile, rows, :] * state + fresh_s[tile, rows, :]
            state_ref[tile, rows, :] = state
            after.append(state)
        return after

    lax.fori_loop(0, size, scan, [carry_s[tile, sub] for tile, sub in lanes], unroll=4)
    ones = jnp.ones((8, 128), F32)

    def gate(slot, _):
        block = nat_ref[slot]
        row = pl.multiple_of(slot * blk, blk)
        out = pl.ds(pl.multiple_of(block * blk, blk), blk)
        held = pl.ds(pl.multiple_of(slot * (blk + GAP), 8), blk)
        square = jnp.zeros((blk, 128), F32)
        for tile in tiles:
            lo = tile * 128
            state = state_ref[tile, held, :]
            pre_g = pre_ref[pl.ds(row, blk), 2 * chans + lo : 2 * chans + lo + 128]
            gated = state * gain_ref[:, lo : lo + 128] * jax.nn.silu(pre_g)
            gated_ref[out, lo : lo + 128] = gated.astype(BF16)
            square += state * state
        sums = lax.dot_general(
            ones,
            square,
            (((1,), (1,)), ((), ())),
            precision=lax.Precision.HIGHEST,
            preferred_element_type=F32,
        )
        square_s[pl.ds(block, 1), :] = sums[:1]
        return 0

    lax.fori_loop(0, nblk, gate, 0)
    high, low = two_terms(square_s[...])
    gated_ref[total:, :128] = jnp.concatenate([high, low], axis=0)
    if chans > 128:
        gated_ref[total:, 128:] = jnp.zeros((2 * nblk, chans - 128), BF16)


def recur_forward(nat, slot, pre, keep, bound, gain, blk):
    chans = bound.shape[1]
    total = keep.shape[0]
    nblk = total // blk
    tiles = chans // 128
    out = jax.ShapeDtypeStruct
    return pl.pallas_call(
        functools.partial(forward_kernel, blk=blk),
        out_shape=(
            out((tiles, nblk * (blk + GAP), 128), F32),
            out((tiles, nblk * (blk + GAP), 128), F32),
            out((total + 2 * nblk, chans), BF16),
        ),
        in_specs=[smem(), smem()] + [vmem()] * 4,
        out_specs=(vmem(),) * 3,
        scratch_shapes=[
            pltpu.VMEM((tiles, nblk * (blk + GAP), 128), F32),
            pltpu.VMEM((tiles, nblk * (blk + GAP), 128), F32),
            pltpu.VMEM((nblk, 128), F32),
            pltpu.VMEM((tiles, SUB, nblk, 128), F32),
            pltpu.VMEM((tiles, SUB, nblk, 128), F32),
            pltpu.VMEM((tiles, SUB, nblk, 128), F32),
        ],
        compiler_params=params(
            [((total, 3 * chans), 4), ((total, 1), 4), ((total + 2 * nblk, chans), 2)]
            + [((tiles, nblk * (blk + GAP), 128), 4)] * 4
        ),
        cost_estimate=cost(total * chans * 30, total * chans * 24, total * chans * 6),
        name="recur_forward",
    )(nat, slot, keep, bound, gain, pre)


def backward_kernel(
    nat_ref, slot_ref, state_ref, prior_ref, keep_ref, bound_ref, gain_ref,
    grad_ref, pre_ref, ext_ref, inv_ref, gpre_ref, gated_ref, gain_sum_ref, bound_sum_ref,
    decay_s, grad_s, prod_s, last_s, carry_s,
    *, blk, width,
):
    chans = bound_ref.shape[1]
    total = gated_ref.shape[0]
    nblk = total // blk
    tiles = range(chans // 128)
    zero_row = jnp.zeros((1, 128), F32)

    def enter(slot, summed):
        at = pl.multiple_of(nat_ref[slot] * blk, blk)
        here = pl.ds(pl.multiple_of(slot * blk, blk), blk)
        held = pl.ds(pl.multiple_of(slot * (blk + GAP), 8), blk)
        ext = ext_ref[here, :].astype(F32)
        inner = (ext[:, 0:1] + ext[:, 1:2]) * (1.0 / width)
        inv = inv_ref[here, 0:1]
        keep = keep_ref[pl.ds(at, blk), :]
        after = []
        for tile in tiles:
            lo = tile * 128
            bound = bound_ref[:, lo : lo + 128]
            gain = gain_ref[:, lo : lo + 128]
            grad = grad_ref[here, lo : lo + 128]
            pre_f = pre_ref[here, chans + lo : chans + lo + 128]
            pre_g = pre_ref[here, 2 * chans + lo : 2 * chans + lo + 128]
            unit = state_ref[tile, held, :] * inv
            sig_g = jax.nn.sigmoid(pre_g)
            act_g = pre_g * sig_g
            scaled = gain * act_g
            grad_s[tile, held, :] = inv * (grad * scaled - unit * inner)
            gated_ref[here, lo : lo + 128] = (unit * scaled).astype(BF16)
            both = grad * unit
            slope = sig_g * (1.0 + pre_g * (1.0 - sig_g))
            gpre_ref[here, 2 * chans + lo : 2 * chans + lo + 128] = (both * gain * slope).astype(
                BF16
            )
            forget = bound + (1.0 - bound) * jax.nn.sigmoid(pre_f)
            decay_s[tile, held, :] = forget * keep
            after.append(summed[tile] + jnp.sum(both * act_g, axis=0, keepdims=True))
        return after

    sums = lax.fori_loop(0, nblk, enter, [zero_row for _ in tiles])
    for tile in tiles:
        gain_sum_ref[:, tile * 128 : tile * 128 + 128] = sums[tile]

    size = blk // SUB
    lanes = [(tile, sub) for tile in tiles for sub in range(SUB)]

    def local(step, carried):
        after = []
        for (tile, sub), (prod, last) in zip(lanes, carried):
            rows = pl.ds((sub + 1) * size - 1 - step, nblk, stride=blk + GAP)
            decay = decay_s[tile, rows, :]
            after.append((prod * decay, decay * (grad_s[tile, rows, :] + last)))
        return after

    shape = (nblk, 128)
    ends = lax.fori_loop(
        0, size, local, [(jnp.ones(shape, F32), jnp.zeros(shape, F32)) for _ in lanes], unroll=4
    )
    for (tile, sub), (prod, last) in zip(lanes, ends):
        prod_s[tile, sub] = prod
        last_s[tile, sub] = last

    def link(step, carry):
        own = pl.ds(slot_ref[nblk - 1 - step], 1)
        after = []
        for tile in tiles:
            back = carry[tile]
            for sub in range(SUB - 1, -1, -1):
                carry_s[tile, sub, own, :] = back
                back = prod_s[tile, sub, own, :] * back + last_s[tile, sub, own, :]
            after.append(back)
        return after

    lax.fori_loop(0, nblk, link, [zero_row for _ in tiles])

    def scan(step, carried):
        after = []
        for (tile, sub), back in zip(lanes, carried):
            rows = pl.ds((sub + 1) * size - 1 - step, nblk, stride=blk + GAP)
            grad = grad_s[tile, rows, :] + back
            grad_s[tile, rows, :] = grad
            after.append(decay_s[tile, rows, :] * grad)
        return after

    lax.fori_loop(0, size, scan, [carry_s[tile, sub] for tile, sub in lanes], unroll=4)

    def leave(slot, summed):
        at = pl.multiple_of(nat_ref[slot] * blk, blk)
        here = pl.ds(pl.multiple_of(slot * blk, blk), blk)
        held = pl.ds(pl.multiple_of(slot * (blk + GAP), 8), blk)
        keep = keep_ref[pl.ds(at, blk), :]
        after = []
        for tile in tiles:
            lo = tile * 128
            bound = bound_ref[:, lo : lo + 128]
            pre_i = pre_ref[here, lo : lo + 128]
            pre_f = pre_ref[here, chans + lo : chans + lo + 128]
            grad = grad_s[tile, held, :]
            sig_i = jax.nn.sigmoid(pre_i)
            sig_f = jax.nn.sigmoid(pre_f)
            forget = bound + (1.0 - bound) * sig_f
            rest = 1.0 - sig_f
            grad_forget = grad * keep * prior_ref[tile, held, :] - grad * (pre_i * sig_i)
            grad_i = grad * (1.0 - forget) * (sig_i * (1.0 + pre_i * (1.0 - sig_i)))
            gpre_ref[here, lo : lo + 128] = grad_i.astype(BF16)
            grad_f = grad_forget * (1.0 - bound) * sig_f * rest
            gpre_ref[here, chans + lo : chans + lo + 128] = grad_f.astype(BF16)
            after.append(summed[tile] + jnp.sum(grad_forget * rest, axis=0, keepdims=True))
        return after

    sums = lax.fori_loop(0, nblk, leave, [zero_row for _ in tiles])
    for tile in tiles:
        bound_sum_ref[:, tile * 128 : tile * 128 + 128] = sums[tile]


def recur_backward(
    nat, slot, grad, pre, ext, inv, state, prior, keep, bound, gain, blk, width
):
    tiles = state.shape[0]
    total = keep.shape[0]
    chans = tiles * 128
    nblk = total // blk
    out = jax.ShapeDtypeStruct
    return pl.pallas_call(
        functools.partial(backward_kernel, blk=blk, width=width),
        out_shape=(
            out((total, 3 * chans), BF16),
            out((total, chans), BF16),
            out((1, chans), F32),
            out((1, chans), F32),
        ),
        in_specs=[smem(), smem()] + [vmem()] * 9,
        out_specs=(vmem(),) * 4,
        scratch_shapes=[
            pltpu.VMEM((tiles, nblk * (blk + GAP), 128), F32),
            pltpu.VMEM((tiles, nblk * (blk + GAP), 128), F32),
            pltpu.VMEM((tiles, SUB, nblk, 128), F32),
            pltpu.VMEM((tiles, SUB, nblk, 128), F32),
            pltpu.VMEM((tiles, SUB, nblk, 128), F32),
        ],
        compiler_params=params(
            [((total, 4 * chans), 4), ((total, 1), 4), ((total, EXT), 4), ((total, EXT), 2)]
            + [((tiles, nblk * (blk + GAP), 128), 4)] * 4
            + [((total, 4 * chans), 2), ((128, width), 4)]
        ),
        cost_estimate=cost(total * chans * 60, total * chans * 36, total * chans * 8),
        name="recur_backward",
    )(nat, slot, state, prior, keep, bound, gain, grad, pre, ext, inv)


def pin(*arrays):
    return [pltpu.with_memory_space_constraint(array, pltpu.HBM) for array in arrays]


def anywhere():
    return pl.BlockSpec(memory_space=pl.ANY)


def part_of(rows, cols, first):
    return pl.BlockSpec((pl.Element(rows), pl.Element(cols)), lambda i: (first, 0))


def pre_kernel(gain_ref, *refs, count):
    blocks, weights = refs[:count], refs[count : count + 3]
    rows_ref, normed_ref, pre_ref, out_w_ref = refs[-4:]
    blk = rows_ref.shape[0] // count
    more = blocks[0].shape[0] - blk
    chans = weights[0].shape[1]
    gain = gain_ref[...]
    for b, block in enumerate(blocks):

        def chunk(step, _, block=block, b=b):
            at = pl.multiple_of(step * 16, 16)
            value = block[pl.ds(at, 16), :]
            out = pl.ds(pl.multiple_of(b * blk + at, 16), 16)
            rows_ref[out, :] = value
            rows = value.astype(F32)
            normed_ref[out, :] = (rows * inverse_rms(rows) * gain).astype(BF16)
            return 0

        lax.fori_loop(0, blk // 16, chunk, 0, unroll=4)
        out_w_ref[b * more : (b + 1) * more, :] = block[blk:, :]
    for k, weight in enumerate(weights):
        pre_ref[:, k * chans : (k + 1) * chans] = dot_nn(normed_ref[...], weight[...])


def make_pre(gain, blocks, weights, held, blk, lo, size, out_lo, out_size):
    both, width = blocks[0].shape
    count = len(blocks)
    rows, more = blk * count, both - blk
    chans = weights[0].shape[1]
    out = jax.ShapeDtypeStruct
    inputs = 4 + count
    there = [k for k, array in enumerate(held) if array is not None]
    return pl.pallas_call(
        functools.partial(pre_kernel, count=count),
        grid=(1,),
        out_shape=(
            pltpu.HBM((size * blk, width), BF16),
            pltpu.HBM((size * blk, width), BF16),
            pltpu.HBM((size * blk, 3 * chans), F32),
            pltpu.HBM((out_size * more, width), BF16),
        ),
        in_specs=[vmem()] * inputs + [anywhere()] * len(there),
        out_specs=(
            part_of(rows, width, lo * blk),
            part_of(rows, width, lo * blk),
            part_of(rows, 3 * chans, lo * blk),
            part_of(more * count, width, (lo - out_lo) * more),
        ),
        input_output_aliases={inputs + n: k for n, k in enumerate(there)},
        compiler_params=params([((rows, width), 2)] * 6 + [((width + 4 * rows, 3 * chans), 2)]),
        cost_estimate=cost(6 * rows * width * chans, rows * width * 6 + 6 * width * chans),
        name="make_pre",
    )(gain, *blocks, *weights, *pin(*(held[k] for k in there)))


def back_kernel(weight_ref, *refs, count):
    blocks, (rows_ref, out_ref) = refs[:count], refs[-2:]
    blk = blocks[0].shape[0]
    for b, block in enumerate(blocks):
        rows_ref[b * blk : (b + 1) * blk, :] = block[...]
    out_ref[...] = dot_nt(rows_ref[...], weight_ref[...])


def make_back(weight, blocks, held, first, total):
    blk, width = blocks[0].shape
    rows, units = blk * len(blocks), weight.shape[0]
    out = jax.ShapeDtypeStruct
    count = 1 + len(blocks)
    return pl.pallas_call(
        functools.partial(back_kernel, count=len(blocks)),
        grid=(1,),
        out_shape=(pltpu.HBM((total, width), BF16), pltpu.HBM((total, units), F32)),
        in_specs=[vmem()] * count + [anywhere()] * len(held),
        out_specs=(part_of(rows, width, first), part_of(rows, units, first)),
        input_output_aliases={count + k: k for k in range(len(held))},
        compiler_params=params([((2 * rows + units, width), 2), ((rows, units), 4)] * 2),
        cost_estimate=cost(2 * rows * width * units, (rows + units) * width * 2),
        name="make_back",
    )(weight, *blocks, *pin(*held))


def gated_grad_kernel(weight_ref, *refs, count):
    blocks, (rows_ref, out_ref, ext_ref) = refs[:count], refs[-3:]
    blk = blocks[0].shape[0]
    width = rows_ref.shape[1]
    for b, block in enumerate(blocks):
        rows_ref[b * blk : (b + 1) * blk, :] = block[:, :width]
        ext_ref[b * blk : (b + 1) * blk, :] = block[:, width:]
    out_ref[...] = dot_nt(rows_ref[...], weight_ref[...])


def make_gated_grad(weight, blocks, held, first, total):
    chans, width = weight.shape
    blk = blocks[0].shape[0]
    rows = blk * len(blocks)
    out = jax.ShapeDtypeStruct
    count = 1 + len(blocks)
    return pl.pallas_call(
        functools.partial(gated_grad_kernel, count=len(blocks)),
        grid=(1,),
        out_shape=(pltpu.HBM((total, width), BF16), pltpu.HBM((total, chans), F32), pltpu.HBM((total, EXT), BF16)),
        in_specs=[vmem()] * count + [anywhere()] * len(held),
        out_specs=(
            part_of(rows, width, first),
            part_of(rows, chans, first),
            part_of(rows, EXT, first),
        ),
        input_output_aliases={count + k: k for k in range(len(held))},
        compiler_params=params([((2 * rows + chans, width + EXT), 2), ((rows, chans), 4)] * 2),
        cost_estimate=cost(2 * rows * width * chans, (rows + chans) * width * 2, scale=0),
        name="make_gated_grad",
    )(weight, *blocks, *pin(*held))


def mix_kernel(at_ref, nat_ref, w_a, w_b, w_c, w_d, *refs, count, held):
    gated, (out_ref, weight_s, gated_s) = refs[:count], refs[-3:]
    chans = gated[0].shape[1]
    rows = chans // 4

    @pl.when(pl.program_id(0) == 0)
    def _():
        for k in range(count):
            for part, weight in enumerate((w_a, w_b, w_c, w_d)):
                to = pl.multiple_of(k * chans + at_ref[part] * rows, rows)
                weight_s[pl.ds(to, rows), :] = weight[k * rows : (k + 1) * rows, :]

    for k in range(count):
        gated_s[:, k * chans : (k + 1) * chans] = gated[k][...]
    tile = 512
    for col in range(0, out_ref.shape[1], tile):
        summed = dot_nn(gated_s[...], weight_s[:, col : col + tile])
        if held:
            summed += refs[count][:, col : col + tile]
        out_ref[:, col : col + tile] = summed


def make_mix(nat, at, gated, weights, held, blk):
    count = len(gated)
    chans = gated[0].shape[1]
    width = weights[0].shape[1]
    nblk = nat.shape[0]
    whole = pl.BlockSpec(weights[0].shape, lambda i, at, nat: (0, 0), pipeline_mode=pl.Buffered(1))
    rows = pl.BlockSpec((blk, width), lambda i, at, nat: (i, 0))
    more = [] if held is None else [held]
    return pl.pallas_call(
        functools.partial(mix_kernel, count=count, held=bool(more)),
        out_shape=pltpu.HBM((nblk * blk, width), F32),
        grid_spec=pltpu.PrefetchScalarGridSpec(
            num_scalar_prefetch=2,
            grid=(nblk,),
            in_specs=[whole] * 4
            + [pl.BlockSpec((blk, chans), lambda i, at, nat: (nat[i], 0))] * count
            + [rows] * len(more),
            out_specs=rows,
            scratch_shapes=[
                pltpu.VMEM((count * chans, width), BF16),
                pltpu.VMEM((blk, count * chans), BF16),
            ],
        ),
        input_output_aliases={6 + count: 0} if more else {},
        compiler_params=params(
            [(weights[0].shape, 2)] * 4
            + [((count * chans, width), 2), ((blk, count * chans), 2)]
            + [((blk, chans), 2)] * (2 * count)
            + [((blk, width), 4)] * 5
        ),
        cost_estimate=cost(
            2 * nblk * blk * count * chans * width,
            count * chans * width * 2 + nblk * blk * (width * 4 + count * chans * 2),
        ),
        name="make_mix",
    )(at, nat, *weights, *gated, *pin(*more))


def glu_kernel(
    nat_ref, at_ref, gated_ref, w_a, w_b, w_c, w_d, mixed_ref, rows_ref, square_ref, gain_ref,
    gate_w_ref, up_w_ref, back_ref, *refs, first, count,
):
    normed_ref, hidden_ref, grad_gate_ref, grad_up_ref, inv_ref, term_ref, *own = refs[count:]
    step = pl.program_id(0)
    blk, width = rows_ref.shape
    *own, weight_s = own

    @pl.when(step == 0)
    def _():
        for part, weight in enumerate((w_a, w_b, w_c, w_d)):
            size = weight.shape[0]
            weight_s[pl.ds(pl.multiple_of(at_ref[part] * size, size), size), :] = weight[...]

    square = square_ref[pl.ds(nat_ref[first + step], 1), :]
    row = lax.broadcasted_iota(jnp.int32, (blk, blk), 0)
    col = lax.broadcasted_iota(jnp.int32, (blk, blk), 1)
    square = jnp.sum(jnp.where(row == col, square, 0.0), axis=1, keepdims=True)
    inv = lax.rsqrt(square / width + EPS)
    mixed = mixed_ref[...] + dot_nn(gated_ref[...], weight_s[...])
    middle = rows_ref[...].astype(F32) + mixed * inv
    inv_two = inverse_rms(middle)
    normed_ref[...] = (middle * inv_two * gain_ref[...]).astype(BF16)
    lane = lax.broadcasted_iota(jnp.int32, (blk, EXT), 1)
    inv_ref[...] = jnp.where(lane == 0, inv, jnp.where(lane == 1, inv_two, 0.0))
    if own:

        @pl.when(step == 0)
        def _():
            own[0][...] = middle

    gate = dot_nt(normed_ref[...], gate_w_ref[...])
    up = dot_nt(normed_ref[...], up_w_ref[...])
    back = back_ref[...]
    sig = jax.nn.sigmoid(gate)
    act = gate * sig
    hidden_ref[...] = (act * up).astype(BF16)
    grad_gate_ref[...] = (back * up * (sig * (1.0 + gate * (1.0 - sig)))).astype(BF16)
    grad_up_ref[...] = (back * act).astype(BF16)
    term_ref[...] = (
        dot_nn(grad_gate_ref[...], gate_w_ref[...]) + dot_nn(grad_up_ref[...], up_w_ref[...])
    ).astype(BF16)


def make_glu(nat, at, gated, weights, mixed, rows, square, gain, gate_w, up_w, back, held, lo, hi):
    total, width = rows.shape
    blk = square.shape[1]
    chans, units = gated.shape[1], gate_w.shape[0]
    out = jax.ShapeDtypeStruct

    def fixed(value):
        return pl.BlockSpec(
            value.shape, lambda i, nat, at: (0,) * value.ndim, pipeline_mode=pl.Buffered(1)
        )

    def tiled(cols, base=lo):
        return pl.BlockSpec((blk, cols), lambda i, nat, at: (base + i, 0))

    shapes = [pltpu.HBM((total, width), BF16)] + [pltpu.HBM((total, units), BF16)] * 3
    shapes += [pltpu.HBM((total, EXT), F32), out(((hi - lo) * blk, width), BF16)]
    specs = [tiled(width)] + [tiled(units)] * 3 + [tiled(EXT), tiled(width, 0)]
    if lo == 0:
        shapes.append(out((blk, width), F32))
        specs.append(pl.BlockSpec((blk, width), lambda i, nat, at: (0, 0)))
    return pl.pallas_call(
        functools.partial(glu_kernel, first=lo, count=len(held)),
        out_shape=shapes,
        grid_spec=pltpu.PrefetchScalarGridSpec(
            num_scalar_prefetch=2,
            grid=(hi - lo,),
            in_specs=[pl.BlockSpec((blk, chans), lambda i, nat, at: (nat[lo + i], 0))]
            + [pl.BlockSpec((chans // 4, width), lambda i, nat, at: (2, 0))] * 4
            + [tiled(width), tiled(width), fixed(square), fixed(gain)]
            + [fixed(gate_w), fixed(up_w), tiled(units)]
            + [anywhere()] * len(held),
            out_specs=specs,
            scratch_shapes=[pltpu.VMEM((chans, width), BF16)],
        ),
        input_output_aliases={14 + k: k for k in range(len(held))},
        compiler_params=params(
            [((chans, width), 2)] * 3
            + [(gate_w.shape, 2)] * 2
            + [((blk, width), 4)] * 12
            + [((blk, units), 4)] * 10
        ),
        cost_estimate=cost(
            (hi - lo) * blk * width * (2 * chans + 8 * units),
            (hi - lo) * blk * width * 8 + 4 * units * width,
        ),
        name="make_glu",
    )(nat, at, *pin(gated, *weights, mixed, rows), square, gain, gate_w, up_w, *pin(back, *held))


def matmul_kernel(lhs_ref, rhs_ref, out_ref):
    out_ref[...] = dot_nn(lhs_ref[...], rhs_ref[...]).astype(out_ref.dtype)


def make_product(lhs, rhs, blk, lo, hi):
    inner, width = rhs.shape
    rows = (hi - lo) * blk
    return pl.pallas_call(
        matmul_kernel,
        grid=(hi - lo,),
        out_shape=jax.ShapeDtypeStruct((rows, width), BF16),
        in_specs=[
            pl.BlockSpec((blk, inner), lambda i: (lo + i, 0)),
            pl.BlockSpec((inner, width), lambda i: (0, 0), pipeline_mode=pl.Buffered(1)),
        ],
        out_specs=pl.BlockSpec((blk, width), lambda i: (i, 0)),
        compiler_params=params([((inner, width), 2)] + [((blk, width + inner), 4)] * 5),
        cost_estimate=cost(2 * rows * inner * width, (rows * inner + (rows + inner) * width) * 2, scale=0),
        name="make_product",
    )(lhs, rhs)


def last_kernel(gpre_ref, w_a, w_b, w_c, normed_ref, term_ref, sum_ref):
    chans = w_a.shape[1]
    total = None
    for k, weight in enumerate((w_a, w_b, w_c)):
        term = dot_nt(gpre_ref[:, k * chans : (k + 1) * chans], weight[...])
        total = term if total is None else total + term
    term_ref[...] = total.astype(BF16)
    part = jnp.sum(total * normed_ref[...].astype(F32), axis=0, keepdims=True)

    @pl.when(pl.program_id(0) == 0)
    def _():
        sum_ref[...] = jnp.zeros_like(sum_ref)

    sum_ref[...] += part


def make_last(gpre, weights, normed, blk, lo, hi):
    width, chans = weights[0].shape
    rows = (hi - lo) * blk
    out = jax.ShapeDtypeStruct
    fixed = pl.BlockSpec((width, chans), lambda i: (0, 0), pipeline_mode=pl.Buffered(1))
    return pl.pallas_call(
        last_kernel,
        grid=(hi - lo,),
        out_shape=(out((rows, width), BF16), out((1, width), F32)),
        in_specs=[pl.BlockSpec((blk, 3 * chans), lambda i: (lo + i, 0))]
        + [fixed] * 3
        + [pl.BlockSpec((blk, width), lambda i: (lo + i, 0))],
        out_specs=(
            pl.BlockSpec((blk, width), lambda i: (i, 0)),
            pl.BlockSpec((1, width), lambda i: (0, 0)),
        ),
        compiler_params=params([((width, chans), 2)] * 3 + [((blk, width), 4)] * 8),
        cost_estimate=cost(6 * rows * width * chans, rows * width * 4 + 6 * width * chans),
        name="make_last",
    )(gpre, *weights, normed)


def middle_grad_kernel(
    r_ref, l_ref, part_ref, rows_ref, middle_ref, inv_ref, cot_ref, weight_ref, gain_ref,
    grad_ref, send_ref, gain_sum_ref,
):
    blk, width = rows_ref.shape
    gain = gain_ref[...]
    weight = weight_ref[0, 0]

    def chunk(step, summed):
        rows = pl.ds(pl.multiple_of(step * 16, 16), 16)
        grad_two = (
            r_ref[rows, :].astype(F32) + l_ref[rows, :].astype(F32) + part_ref[rows, :].astype(F32)
        )
        inv_two = inv_ref[rows, 1:2]
        middle = middle_ref[rows, :]
        unit = middle * inv_two
        scaled = grad_two * gain
        mean = jnp.mean(scaled * unit, axis=1, keepdims=True)
        grad = cot_ref[rows, :].astype(F32) * weight + inv_two * (scaled - unit * mean)
        grad_ref[rows, :] = grad
        sent = grad.astype(BF16)
        send_ref[rows, :width] = sent
        mix = middle - rows_ref[rows, :].astype(F32)
        inner = jnp.sum(sent.astype(F32) * mix, axis=1, keepdims=True)
        high, low = two_terms(inner)
        lane = lax.broadcasted_iota(jnp.int32, (16, EXT), 1)
        ext = jnp.where(
            lane == 0, high.astype(F32), jnp.where(lane == 1, low.astype(F32), 0.0)
        )
        send_ref[rows, width:] = ext.astype(BF16)
        return summed + jnp.sum(grad_two * unit, axis=0, keepdims=True)

    gain_sum_ref[...] = lax.fori_loop(0, blk // 16, chunk, jnp.zeros((1, width), F32))


def make_middle_grad(r_in, l_in, part, rows, middle, inv, cot, weight, gain):
    blk, width = rows.shape
    out = jax.ShapeDtypeStruct
    return pl.pallas_call(
        middle_grad_kernel,
        grid=(1,),
        out_shape=(
            out((blk, width), F32),
            out((blk, width + EXT), BF16),
            out((1, width), F32),
        ),
        in_specs=[vmem(), vmem(), pl.BlockSpec((blk, width), lambda i: (0, 0))]
        + [vmem()] * 2
        + [pl.BlockSpec((blk, EXT), lambda i: (0, 0)), vmem()]
        + [smem(), vmem()],
        out_specs=(vmem(),) * 3,
        compiler_params=params([((blk, width + EXT), 4)] * 6),
        cost_estimate=cost(blk * width * 16, blk * width * 20, scale=0),
        name="make_middle_grad",
    )(r_in, l_in, part, rows, middle, inv, cot, weight, gain)


def final_kernel(
    r_ref, l_ref, part_ref, rows_ref, grad_ref, gain_ref, out_ref,
):
    blk = rows_ref.shape[0]
    gain = gain_ref[...]

    def chunk(step, _):
        at = pl.multiple_of(step * 16, 16)
        rows = pl.ds(at, 16)
        grad = (
            r_ref[rows, :].astype(F32) + l_ref[rows, :].astype(F32) + part_ref[rows, :].astype(F32)
        )
        own = rows_ref[rows, :].astype(F32)
        inv = inverse_rms(own)
        unit = own * inv
        scaled = grad * gain
        mean = jnp.mean(scaled * unit, axis=1, keepdims=True)
        out_ref[rows, :] = grad_ref[rows, :] + inv * (scaled - unit * mean)
        return 0

    lax.fori_loop(0, blk // 16, chunk, 0)


def make_final(r_in, l_in, part, rows, grad, gain):
    blk, width = rows.shape
    return pl.pallas_call(
        final_kernel,
        out_shape=jax.ShapeDtypeStruct((blk, width), F32),
        in_specs=[vmem()] * 6,
        out_specs=vmem(),
        compiler_params=params([((blk, width), 4)] * 8),
        cost_estimate=cost(blk * width * 16, blk * width * 18),
        name="make_final",
    )(r_in, l_in, part, rows, grad, gain)


class Ring:
    def __init__(self, size):
        self.size = size
        self.steps = size // 2
        order = list(range(0, size, 2)) + list(range(size - 1, 0, -2))
        place = {device: at for at, device in enumerate(order)}
        self.right = [(order[i], order[(i + 1) % size]) for i in range(size)]
        self.left = [(b, a) for a, b in self.right]
        offs = [0]
        for k in range(1, self.steps):
            offs += [-k, k]
        offs.append(self.steps)
        cuts = [0, *range(3, size, 2), size]
        self.spans = list(zip(cuts[:-1], cuts[1:]))
        self.pairs = [(0, 1), (1, 3), *self.spans[1:]]
        nat = np.zeros((size, size), np.int32)
        slot = np.zeros((size, size), np.int32)
        for device in range(size):
            for at, off in enumerate(offs):
                block = order[(place[device] + off) % size]
                nat[device, at] = block
                slot[device, block] = at
        self.nat, self.slot = nat, slot

    def move(self, right, left):
        return lax.ppermute(right, "mp", self.right), lax.ppermute(left, "mp", self.left)

    def gather(self, k, pair):
        right, left = pair
        if k == self.steps - 1:
            rows = right.shape[0] // 32 * 16
            return self.move(right[:rows], left[rows:])
        return self.move(right, left)

    def scatter(self, k, pair, group):
        if k == 0:
            rows = group.shape[0] // 2
            return self.move(group[:rows], group[rows:])
        right, left = pair
        blk = group.shape[0] // 2
        to_left, to_right = group[:blk], group[blk:]
        if k == 1:
            rows = blk // 2
            right = jnp.concatenate([add(right, to_right[:rows]), to_right[rows:]], axis=0)
            left = jnp.concatenate([to_left[:rows], add(left, to_left[rows:])], axis=0)
        else:
            right, left = add(right, to_right), add(left, to_left)
        return self.move(right, left)


def close(*values):
    return lax.optimization_barrier(values)


def add(a, b):
    return (a.astype(F32) + b.astype(F32)).astype(BF16)


def dp_swap(value, bit):
    return lax.ppermute(value, "dp", [(i, i ^ bit) for i in range(lax.axis_size("dp"))])


def mp_swap(value, bit):
    return lax.ppermute(value, "mp", [(i, i ^ bit) for i in range(lax.axis_size("mp"))])


def local(
    block_input,
    out_cotangent,
    segments,
    domain_tags,
    counts,
    attn_gain,
    mlp_gain,
    norm_gain,
    bound_table,
    w_input,
    w_forget,
    w_gate_mix,
    w_out,
    w_glu_gate,
    w_glu_up,
    w_glu_down,
):
    blk, width = block_input.shape
    chans = w_input.shape[1]
    seqs = segments.shape[0]
    total = seqs * LEN
    mp_size, dp_size = lax.axis_size("mp"), lax.axis_size("dp")
    mp_index, dp_index = lax.axis_index("mp"), lax.axis_index("dp")
    ring = Ring(mp_size)
    spans, steps = ring.spans, ring.steps
    last = steps - 1
    nat = lax.dynamic_index_in_dim(jnp.asarray(ring.nat), mp_index, 0, keepdims=False)
    slot = lax.dynamic_index_in_dim(jnp.asarray(ring.slot), mp_index, 0, keepdims=False)
    at = dp_index ^ jnp.array([0, 2, 1, 3], jnp.int32)

    lanes = -(-chans // 128) * 128
    pad = lanes - chans

    def pad_cols(array):
        return jnp.pad(array, ((0, 0), (0, pad))) if pad else array

    mix_weights = [pad_cols(w_input), pad_cols(w_forget), pad_cols(w_gate_mix)]
    w_out_pad = jnp.pad(w_out, ((0, pad), (0, 0))) if pad else w_out
    attn_row, mlp_row = attn_gain[None, :], mlp_gain[None, :]
    gate_w, up_w = w_glu_gate.T, w_glu_up.T

    layer_ids = jnp.arange(NLAYER)
    pick = ((layer_ids >= 1) & (layer_ids <= LAYER)).astype(F32)[:, None]
    bound = pad_cols(jnp.sum(jax.nn.softmax(bound_table, axis=0) * pick, axis=0)[None, :])
    gain = pad_cols(norm_gain[None, :])
    keep = jnp.concatenate(
        [jnp.zeros((seqs, 1), F32), (segments[:, 1:] == segments[:, :-1]).astype(F32)], axis=1
    ).reshape(total, 1)
    seq_count = jnp.sum(
        jnp.where(
            domain_tags[:, None] == jnp.arange(NDOM)[None, :], counts.astype(F32)[None, :], 0.0
        ),
        axis=1,
    )
    weight = lax.dynamic_slice_in_dim(lax.rsqrt(seq_count), mp_index * blk // LEN, 1, 0)
    grad_b = (out_cotangent.astype(F32) * weight[:, None]).astype(BF16)


    quarter = lax.dynamic_slice_in_dim(w_out_pad, dp_index * (lanes // 4), lanes // 4, axis=0)
    own = jnp.concatenate([block_input, quarter], axis=0)
    pair, waiting, held = (own, own), [own], (None,) * 4
    table = bound_table[None]
    split = spans[last - 1][0]

    def pre_group(blocks, held, g):
        part = (split, mp_size - split) if spans[g][0] >= split else (0, split)
        return make_pre(attn_row, blocks, mix_weights, held, blk, spans[g][0], mp_size, *part)

    for k in range(steps):
        pair = ring.gather(k, pair)
        if k == 0:
            more = mp_swap(table, 1)
            pair, bound, keep, grad_b, nat, slot, at = close(
                pair, bound, keep, grad_b, nat, slot, at
            )
            waiting += pair
            continue
        held = pre_group(waiting, held, k - 1)
        if k == 1:
            pair, held, more = close(pair, held, more)
            table = jnp.concatenate([table, more], axis=0)
        elif k < last:
            if k == last - 1:
                *held, out_own = held
                near = [out_own, dp_swap(out_own, 2), dp_swap(out_own, 1)]
                more = mp_swap(table, 2)
                pair, held, near[2], grad_b = close(pair, held, near[2], grad_b)
                held = (*held, None)
            else:
                pair, held = close(pair, held)
        else:
            cot = ring.gather(0, (grad_b, grad_b))
            pair, held, more, near[1] = close(pair, held, more, near[1])
            table = jnp.concatenate([table, more], axis=0)
        waiting = list(pair) if k < last else [jnp.concatenate(pair, axis=0)]
    rows, normed, pre, out_own = pre_group(waiting, held, last)

    near.append(dp_swap(near[1], 1))
    far = [out_own, dp_swap(out_own, 2), dp_swap(out_own, 1)]
    state, prior, gated_own = recur_forward(nat, slot, pre, keep, bound, gain, blk)
    gated_own, cot = close(gated_own, cot)
    pair, gated_blocks, mixed = (gated_own, gated_own), [gated_own], None
    held, cot_waiting = (), [grad_b]
    for k in range(steps):
        pair = ring.gather(k, pair)
        if k == 0:
            pair, near, far[2], cot = close(pair, near, far[2], cot)
            cot_waiting += cot
        else:
            cot = ring.gather(k, cot)
            held = make_back(w_glu_down, cot_waiting, held, spans[k - 1][0] * blk, total)
            if k < last:
                if k == last - 1:
                    mixed = make_mix(nat, at, gated_blocks, near, None, blk)
                    pair, cot, held, mixed, far[1] = close(pair, cot, held, mixed, far[1])
                    far.append(dp_swap(far[1], 1))
                else:
                    pair, cot, held = close(pair, cot, held)
            else:
                mixed = make_mix(nat, at, gated_blocks[split:], far, mixed, blk)
                pair, cot, held, mixed = close(pair, cot, held, mixed)
            cot_waiting = list(cot) if k < last else [jnp.concatenate(cot, axis=0)]
        gated_blocks += pair if k < last else [jnp.concatenate(pair, axis=0)]
    cot_all, back = make_back(w_glu_down, cot_waiting, held, spans[last][0] * blk, total)
    squares = sum(block[total:, :128].astype(F32) for block in gated_blocks)
    squares = squares[:mp_size] + squares[mp_size:]

    pairs = ring.pairs

    def glu_group(held, g):
        weights = pin(gate_w, up_w) if g in (0, last - 1) else (gate_w, up_w)
        return make_glu(
            nat, at, gated_blocks[-1], far, mixed, rows, squares, mlp_row, *weights,
            back, held, *pairs[g],
        )

    def out_group(g):
        return make_product(hidden, w_glu_down, blk, *pairs[g])

    made = glu_group((), steps)
    held, term = made[:5], made[5]
    for k in range(steps):
        pair = ring.scatter(k, pair, term)
        made = glu_group(held, last - k)
        held, term = made[:5], made[5]
        if 4 << k < mp_size:
            more = mp_swap(table, 4 << k)
            pair, held, term, more = close(pair, held, term, more)
            table = jnp.concatenate([table, more], axis=0)
        elif k == last - 1:
            table = jnp.take(table, jnp.arange(mp_size) ^ mp_index, axis=0)
            shares = jax.nn.softmax(table.transpose(1, 0, 2).reshape(NLAYER, width), axis=0)
            pair, held, term, shares = close(pair, held, term, shares)
        else:
            pair, held, term = close(pair, held, term)
    two, hidden, grad_gate, grad_up, inv = held
    middle = made[6]
    outs = [None] * (steps + 1)
    outs[steps] = out_group(steps)
    grad_middle, sent, mlp_term = make_middle_grad(
        *pair, term, block_input, middle, inv, out_cotangent, weight[:, None], mlp_row
    )

    size = width // dp_size

    def cols(array, bits):
        return lax.dynamic_slice_in_dim(array, (dp_index ^ bits) * size, size, axis=1)

    def far_slice(own, rest):
        return (own[0] + rest[0].astype(F32)).astype(BF16)

    def slice_sum(own, rest, far):
        return own[1] + rest[1].astype(F32) + far.astype(F32)

    def slices(left, right, which, split_left=False):
        found = []
        for bits in ((3, 1) if which == "rest" else (2, 0)):
            if split_left:
                found.append(dot_tn(cols(left, bits), right))
            else:
                found.append(dot_tn(left, cols(right, bits)))
        return jnp.stack([value.astype(BF16) for value in found]) if which == "rest" else found

    sent, hidden, two, cot_all, grad_gate, grad_up = close(
        sent, hidden, two, cot_all, grad_gate, grad_up
    )
    pair, res, sent_waiting, held = (sent, sent), (), [sent], ()
    for k in range(steps):
        pair = ring.gather(k, pair)
        res = ring.scatter(k, res, outs[steps - k])
        outs[last - k] = out_group(last - k)
        if k:
            held = make_gated_grad(w_out_pad, sent_waiting, held, spans[k - 1][0] * blk, total)
        if k == 0:
            down = slices(hidden, cot_all, "rest"), slices(hidden, cot_all, "own")
            pair, res, outs[last], down, two, hidden = close(
                pair, res, outs[last], down, two, hidden
            )
            sent_waiting += pair
            continue
        if k == 1:
            down_rest = dp_swap(down[0], 1)
            gate = slices(grad_gate, two, "rest"), slices(grad_gate, two, "own")
            pair, res, outs, held, down_rest, gate, two, hidden = close(
                pair, res, outs, held, down_rest, gate, two, hidden
            )
        elif k == 2:
            down_far = dp_swap(far_slice(down[1], down_rest), 2)
            gate_rest = dp_swap(gate[0], 1)
            up = slices(grad_up, two, "rest"), slices(grad_up, two, "own")
            pair, res, outs, held, gate_rest, up, hidden = close(
                pair, res, outs, held, gate_rest, up, hidden
            )
        elif k < last:
            pair, res, outs, held = close(pair, res, outs, held)
        if k == last:
            up_rest = dp_swap(up[0], 1)
            pair, held, up_rest, outs[0] = close(pair, held, up_rest, outs[0])
        sent_waiting = list(pair) if k < last else [jnp.concatenate(pair, axis=0)]
    sent_all, grad, ext = make_gated_grad(
        w_out_pad, sent_waiting, held, spans[last][0] * blk, total
    )

    grad_pre, gated, norm_term, bound_grad = recur_backward(
        nat, slot, grad, pre, ext, inv, state, prior, keep, bound, gain, blk, width
    )

    def last_group(g, grad_pre):
        return make_last(grad_pre, mix_weights, normed, blk, *pairs[g])

    def placed(row):
        wide = jnp.zeros((1, width), F32)
        return lax.dynamic_update_slice(wide, row[:, :chans], (0, mp_index * chans))

    lasts = [None] * (steps + 1)
    lasts[steps] = last_group(steps, grad_pre)
    for k in range(steps):
        pair = ring.scatter(k, pair, lasts[steps - k][0])
        if k == 0:
            gate_far = dp_swap(far_slice(gate[1], gate_rest), 2)
            lasts[last] = last_group(last, grad_pre)
            mix_rest = slices(normed, grad_pre, "rest", True)
            pair, res, lasts[last], mix_rest, grad_pre, normed, gated, sent_all, down_far, up = close(
                pair, res, lasts[last], mix_rest, grad_pre, normed, gated, sent_all, down_far, up
            )
        elif k == 1:
            mix_rest = dp_swap(mix_rest, 1)
            up_far = dp_swap(far_slice(up[1], up_rest), 2)
            for g in range(last):
                lasts[g] = last_group(g, grad_pre)
            mix = slices(normed, grad_pre, "own", True)
            down, res, outs[0] = close(down, res, outs[0])
            pair, lasts, mix_rest, mix, gated, sent_all, gate_far, down, res, up = close(
                pair, lasts, mix_rest, mix, gated, sent_all, gate_far, down, res, up
            )
        elif k == 2:
            mix_far = dp_swap(far_slice(mix, mix_rest), 2)
            out = slices(gated, sent_all, "rest"), slices(gated, sent_all, "own")
            down_grad = slice_sum(down[1], down_rest, down_far)
            result = (
                middle + res[0].astype(F32) + res[1].astype(F32) + outs[0].astype(F32)
            ).astype(BF16)

            attn_term = sum(found[1] for found in lasts) / attn_row
            packed = jnp.concatenate(
                [attn_term, mlp_term, placed(norm_term), placed(bound_grad)], axis=0
            ).reshape(-1, 128)
            packed = packed + dp_swap(packed, 1)
            packed = packed + mp_swap(packed, 1)
            pair, out, down_grad, result, packed, gate, up, up_far = close(
                pair, out, down_grad, result, packed, gate, up, up_far
            )
        elif k < last:
            (pair,) = close(pair)
        else:
            out_rest = dp_swap(out[0], 1)
            packed = packed + mp_swap(packed, 2)
            packed = packed + dp_swap(packed, 2)
            glu_gate_grad = slice_sum(gate[1], gate_rest, gate_far)
            glu_up_grad = slice_sum(up[1], up_rest, up_far)
            pair, packed, out_rest, glu_gate_grad, glu_up_grad, mix_far = close(
                pair, packed, out_rest, glu_gate_grad, glu_up_grad, mix_far
            )
    out_far = dp_swap(far_slice(out[1], out_rest), 2)
    reach = 4
    while reach < mp_size:
        packed = packed + mp_swap(packed, reach)
        reach *= 2
    grad_block_input = make_final(*pair, lasts[0][0], block_input, grad_middle, attn_row)
    mix_grad = slice_sum(mix, mix_rest, mix_far)
    out_grad = slice_sum(out[1], out_rest, out_far)[:chans]
    glu_gate_grad, glu_up_grad = glu_gate_grad.T, glu_up_grad.T

    attn_sum, mlp_sum, norm_sum, bound_sum = packed.reshape(4, width)
    pick_grad = pick * bound_sum[None, :]
    table_sum = shares * (pick_grad - jnp.sum(shares * pick_grad, axis=0, keepdims=True))
    return (
        result,
        grad_block_input,
        attn_sum,
        mlp_sum,
        norm_sum,
        table_sum,
        mix_grad[:, :chans],
        mix_grad[:, lanes : lanes + chans],
        mix_grad[:, 2 * lanes : 2 * lanes + chans],
        out_grad,
        glu_gate_grad,
        glu_up_grad,
        down_grad,
    )


def solution(mesh):
    placed = (
        P(("dp", "mp"), None),
        P(("dp", "mp"), None),
        P("dp", None),
        P("dp"),
        P(),
        P(),
        P(),
        P("mp"),
        P(None, "mp"),
        P(None, "mp"),
        P(None, "mp"),
        P(None, "mp"),
        P("mp", None),
        P(None, "mp"),
        P(None, "mp"),
        P("mp", None),
    )
    return jax.shard_map(
        local,
        mesh=mesh,
        in_specs=placed,
        out_specs=(
            P(("dp", "mp"), None),
            P(("dp", "mp"), None),
            P(),
            P(),
            P(),
            P(),
            P("dp", "mp"),
            P("dp", "mp"),
            P("dp", "mp"),
            P("mp", "dp"),
            P("dp", "mp"),
            P("dp", "mp"),
            P("mp", "dp"),
        ),
        check_vma=False,
    )
```

```python
import functools

import jax
import jax.numpy as jnp
import numpy as np
from jax import lax
from jax.experimental import pallas as pl
from jax.experimental.pallas import tpu as pltpu
from jax.sharding import PartitionSpec as P

NLAYER = 24
LAYER = 20
LEN = 1024
NDOM = 8
EXT = 128
SUB = 4
GAP = 8
EPS = 1e-06
F32 = jnp.float32
BF16 = jnp.bfloat16
MIB = 1 << 20
GRANT = 0


def vmem():
    return pl.BlockSpec(memory_space=pltpu.VMEM)


def smem():
    return pl.BlockSpec(memory_space=pltpu.SMEM)


def params(arrays, least=GRANT):
    used = 0
    for shape, item in arrays:
        lead = int(np.prod(shape[:-2])) if len(shape) > 2 else 1
        used += lead * (-(-shape[-2] // 16) * 16) * (-(-shape[-1] // 128) * 128) * item
    return pltpu.CompilerParams(vmem_limit_bytes=max(used + used // 8 + 2 * MIB, least * MIB))


def tie(value, *after):
    return lax.optimization_barrier((value, *after))[0]


def cost(flops, nbytes, trans=0, scale=1):
    return pl.CostEstimate(
        flops=scale * flops, bytes_accessed=scale * nbytes, transcendentals=scale * trans
    )


def joined(refs):
    return refs[0][...] if len(refs) == 1 else jnp.concatenate([ref[...] for ref in refs], axis=0)


def dot_tn(lhs, rhs):
    return lax.dot_general(lhs, rhs, (((0,), (0,)), ((), ())), preferred_element_type=F32)


def dot_nt(lhs, rhs):
    return lax.dot_general(lhs, rhs, (((1,), (1,)), ((), ())), preferred_element_type=F32)


def dot_nn(lhs, rhs):
    return jnp.dot(lhs, rhs, preferred_element_type=F32)


def inverse_rms(rows):
    return lax.rsqrt(jnp.mean(rows * rows, axis=1, keepdims=True) + EPS)


def two_terms(value):
    high = value.astype(BF16)
    return high, (value - high.astype(F32)).astype(BF16)


def forward_kernel(
    nat_ref, slot_ref, keep_ref, bound_ref, gain_ref, pre_ref,
    state_ref, prior_ref, gated_ref, decay_s, fresh_s, square_s, prod_s, last_s, carry_s,
    *, blk,
):
    chans = bound_ref.shape[1]
    total = keep_ref.shape[0]
    nblk = total // blk
    tiles = range(chans // 128)

    def gates(slot, _):
        at = pl.multiple_of(nat_ref[slot] * blk, blk)
        row = pl.multiple_of(slot * blk, blk)
        out = pl.ds(pl.multiple_of(slot * (blk + GAP), 8), blk)
        keep = keep_ref[pl.ds(at, blk), :]
        for tile in tiles:
            lo = tile * 128
            bound = bound_ref[:, lo : lo + 128]
            pre_i = pre_ref[pl.ds(row, blk), lo : lo + 128]
            pre_f = pre_ref[pl.ds(row, blk), chans + lo : chans + lo + 128]
            forget = bound + (1.0 - bound) * jax.nn.sigmoid(pre_f)
            decay_s[tile, out, :] = forget * keep
            fresh_s[tile, out, :] = jax.nn.silu(pre_i) * (1.0 - forget)
        return 0

    lax.fori_loop(0, nblk, gates, 0)
    size = blk // SUB
    lanes = [(tile, sub) for tile in tiles for sub in range(SUB)]

    def local(pos, carried):
        after = []
        for (tile, sub), (prod, last) in zip(lanes, carried):
            rows = pl.ds(sub * size + pos, nblk, stride=blk + GAP)
            decay = decay_s[tile, rows, :]
            after.append((prod * decay, decay * last + fresh_s[tile, rows, :]))
        return after

    shape = (nblk, 128)
    ends = lax.fori_loop(
        0, size, local, [(jnp.ones(shape, F32), jnp.zeros(shape, F32)) for _ in lanes], unroll=4
    )
    for (tile, sub), (prod, last) in zip(lanes, ends):
        prod_s[tile, sub] = prod
        last_s[tile, sub] = last

    def link(block, carry):
        own = pl.ds(slot_ref[block], 1)
        after = []
        for tile in tiles:
            state = carry[tile]
            for sub in range(SUB):
                carry_s[tile, sub, own, :] = state
                state = prod_s[tile, sub, own, :] * state + last_s[tile, sub, own, :]
            after.append(state)
        return after

    lax.fori_loop(0, nblk, link, [jnp.zeros((1, 128), F32) for _ in tiles])

    def scan(pos, states):
        after = []
        for (tile, sub), state in zip(lanes, states):
            rows = pl.ds(sub * size + pos, nblk, stride=blk + GAP)
            prior_ref[tile, rows, :] = state
            state = decay_s[tile, rows, :] * state + fresh_s[tile, rows, :]
            state_ref[tile, rows, :] = state
            after.append(state)
        return after

    lax.fori_loop(0, size, scan, [carry_s[tile, sub] for tile, sub in lanes], unroll=4)
    ones = jnp.ones((8, 128), F32)

    def gate(slot, _):
        block = nat_ref[slot]
        row = pl.multiple_of(slot * blk, blk)
        out = pl.ds(pl.multiple_of(block * blk, blk), blk)
        held = pl.ds(pl.multiple_of(slot * (blk + GAP), 8), blk)
        square = jnp.zeros((blk, 128), F32)
        for tile in tiles:
            lo = tile * 128
            state = state_ref[tile, held, :]
            pre_g = pre_ref[pl.ds(row, blk), 2 * chans + lo : 2 * chans + lo + 128]
            gated = state * gain_ref[:, lo : lo + 128] * jax.nn.silu(pre_g)
            gated_ref[out, lo : lo + 128] = gated.astype(BF16)
            square += state * state
        sums = lax.dot_general(
            ones,
            square,
            (((1,), (1,)), ((), ())),
            precision=lax.Precision.HIGHEST,
            preferred_element_type=F32,
        )
        square_s[pl.ds(block, 1), :] = sums[:1]
        return 0

    lax.fori_loop(0, nblk, gate, 0)
    high, low = two_terms(square_s[...])
    gated_ref[total:, :128] = jnp.concatenate([high, low], axis=0)
    if chans > 128:
        gated_ref[total:, 128:] = jnp.zeros((2 * nblk, chans - 128), BF16)


def recur_forward(nat, slot, pre, keep, bound, gain, blk):
    chans = bound.shape[1]
    total = keep.shape[0]
    nblk = total // blk
    tiles = chans // 128
    out = jax.ShapeDtypeStruct
    return pl.pallas_call(
        functools.partial(forward_kernel, blk=blk),
        out_shape=(
            out((tiles, nblk * (blk + GAP), 128), F32),
            out((tiles, nblk * (blk + GAP), 128), F32),
            out((total + 2 * nblk, chans), BF16),
        ),
        in_specs=[smem(), smem()] + [vmem()] * 4,
        out_specs=(vmem(),) * 3,
        scratch_shapes=[
            pltpu.VMEM((tiles, nblk * (blk + GAP), 128), F32),
            pltpu.VMEM((tiles, nblk * (blk + GAP), 128), F32),
            pltpu.VMEM((nblk, 128), F32),
            pltpu.VMEM((tiles, SUB, nblk, 128), F32),
            pltpu.VMEM((tiles, SUB, nblk, 128), F32),
            pltpu.VMEM((tiles, SUB, nblk, 128), F32),
        ],
        compiler_params=params(
            [((total, 3 * chans), 4), ((total, 1), 4), ((total + 2 * nblk, chans), 2)]
            + [((tiles, nblk * (blk + GAP), 128), 4)] * 4
        ),
        cost_estimate=cost(total * chans * 30, total * chans * 24, total * chans * 6),
        name="recur_forward",
    )(nat, slot, keep, bound, gain, pre)


def backward_kernel(
    nat_ref, slot_ref, state_ref, prior_ref, keep_ref, bound_ref, gain_ref,
    grad_ref, pre_ref, ext_ref, inv_ref, gpre_ref, gated_ref, gain_sum_ref, bound_sum_ref,
    decay_s, grad_s, prod_s, last_s, carry_s,
    *, blk, width,
):
    chans = bound_ref.shape[1]
    total = gated_ref.shape[0]
    nblk = total // blk
    tiles = range(chans // 128)
    zero_row = jnp.zeros((1, 128), F32)

    def enter(slot, summed):
        at = pl.multiple_of(nat_ref[slot] * blk, blk)
        here = pl.ds(pl.multiple_of(slot * blk, blk), blk)
        held = pl.ds(pl.multiple_of(slot * (blk + GAP), 8), blk)
        ext = ext_ref[here, :].astype(F32)
        inner = (ext[:, 0:1] + ext[:, 1:2]) * (1.0 / width)
        inv = inv_ref[here, 0:1]
        keep = keep_ref[pl.ds(at, blk), :]
        after = []
        for tile in tiles:
            lo = tile * 128
            bound = bound_ref[:, lo : lo + 128]
            gain = gain_ref[:, lo : lo + 128]
            grad = grad_ref[here, lo : lo + 128]
            pre_f = pre_ref[here, chans + lo : chans + lo + 128]
            pre_g = pre_ref[here, 2 * chans + lo : 2 * chans + lo + 128]
            unit = state_ref[tile, held, :] * inv
            sig_g = jax.nn.sigmoid(pre_g)
            act_g = pre_g * sig_g
            scaled = gain * act_g
            grad_s[tile, held, :] = inv * (grad * scaled - unit * inner)
            gated_ref[here, lo : lo + 128] = (unit * scaled).astype(BF16)
            both = grad * unit
            slope = sig_g * (1.0 + pre_g * (1.0 - sig_g))
            gpre_ref[here, 2 * chans + lo : 2 * chans + lo + 128] = (both * gain * slope).astype(
                BF16
            )
            forget = bound + (1.0 - bound) * jax.nn.sigmoid(pre_f)
            decay_s[tile, held, :] = forget * keep
            after.append(summed[tile] + jnp.sum(both * act_g, axis=0, keepdims=True))
        return after

    sums = lax.fori_loop(0, nblk, enter, [zero_row for _ in tiles])
    for tile in tiles:
        gain_sum_ref[:, tile * 128 : tile * 128 + 128] = sums[tile]

    size = blk // SUB
    lanes = [(tile, sub) for tile in tiles for sub in range(SUB)]

    def local(step, carried):
        after = []
        for (tile, sub), (prod, last) in zip(lanes, carried):
            rows = pl.ds((sub + 1) * size - 1 - step, nblk, stride=blk + GAP)
            decay = decay_s[tile, rows, :]
            after.append((prod * decay, decay * (grad_s[tile, rows, :] + last)))
        return after

    shape = (nblk, 128)
    ends = lax.fori_loop(
        0, size, local, [(jnp.ones(shape, F32), jnp.zeros(shape, F32)) for _ in lanes], unroll=4
    )
    for (tile, sub), (prod, last) in zip(lanes, ends):
        prod_s[tile, sub] = prod
        last_s[tile, sub] = last

    def link(step, carry):
        own = pl.ds(slot_ref[nblk - 1 - step], 1)
        after = []
        for tile in tiles:
            back = carry[tile]
            for sub in range(SUB - 1, -1, -1):
                carry_s[tile, sub, own, :] = back
                back = prod_s[tile, sub, own, :] * back + last_s[tile, sub, own, :]
            after.append(back)
        return after

    lax.fori_loop(0, nblk, link, [zero_row for _ in tiles])

    def scan(step, carried):
        after = []
        for (tile, sub), back in zip(lanes, carried):
            rows = pl.ds((sub + 1) * size - 1 - step, nblk, stride=blk + GAP)
            grad = grad_s[tile, rows, :] + back
            grad_s[tile, rows, :] = grad
            after.append(decay_s[tile, rows, :] * grad)
        return after

    lax.fori_loop(0, size, scan, [carry_s[tile, sub] for tile, sub in lanes], unroll=4)

    def leave(slot, summed):
        at = pl.multiple_of(nat_ref[slot] * blk, blk)
        here = pl.ds(pl.multiple_of(slot * blk, blk), blk)
        held = pl.ds(pl.multiple_of(slot * (blk + GAP), 8), blk)
        keep = keep_ref[pl.ds(at, blk), :]
        after = []
        for tile in tiles:
            lo = tile * 128
            bound = bound_ref[:, lo : lo + 128]
            pre_i = pre_ref[here, lo : lo + 128]
            pre_f = pre_ref[here, chans + lo : chans + lo + 128]
            grad = grad_s[tile, held, :]
            sig_i = jax.nn.sigmoid(pre_i)
            sig_f = jax.nn.sigmoid(pre_f)
            forget = bound + (1.0 - bound) * sig_f
            rest = 1.0 - sig_f
            grad_forget = grad * keep * prior_ref[tile, held, :] - grad * (pre_i * sig_i)
            grad_i = grad * (1.0 - forget) * (sig_i * (1.0 + pre_i * (1.0 - sig_i)))
            gpre_ref[here, lo : lo + 128] = grad_i.astype(BF16)
            grad_f = grad_forget * (1.0 - bound) * sig_f * rest
            gpre_ref[here, chans + lo : chans + lo + 128] = grad_f.astype(BF16)
            after.append(summed[tile] + jnp.sum(grad_forget * rest, axis=0, keepdims=True))
        return after

    sums = lax.fori_loop(0, nblk, leave, [zero_row for _ in tiles])
    for tile in tiles:
        bound_sum_ref[:, tile * 128 : tile * 128 + 128] = sums[tile]


def recur_backward(
    nat, slot, grad, pre, ext, inv, state, prior, keep, bound, gain, blk, width
):
    tiles = state.shape[0]
    total = keep.shape[0]
    chans = tiles * 128
    nblk = total // blk
    out = jax.ShapeDtypeStruct
    return pl.pallas_call(
        functools.partial(backward_kernel, blk=blk, width=width),
        out_shape=(
            out((total, 3 * chans), BF16),
            out((total, chans), BF16),
            out((1, chans), F32),
            out((1, chans), F32),
        ),
        in_specs=[smem(), smem()] + [vmem()] * 9,
        out_specs=(vmem(),) * 4,
        scratch_shapes=[
            pltpu.VMEM((tiles, nblk * (blk + GAP), 128), F32),
            pltpu.VMEM((tiles, nblk * (blk + GAP), 128), F32),
            pltpu.VMEM((tiles, SUB, nblk, 128), F32),
            pltpu.VMEM((tiles, SUB, nblk, 128), F32),
            pltpu.VMEM((tiles, SUB, nblk, 128), F32),
        ],
        compiler_params=params(
            [((total, 4 * chans), 4), ((total, 1), 4), ((total, EXT), 4), ((total, EXT), 2)]
            + [((tiles, nblk * (blk + GAP), 128), 4)] * 4
            + [((total, 4 * chans), 2), ((128, width), 4)]
        ),
        cost_estimate=cost(total * chans * 60, total * chans * 36, total * chans * 8),
        name="recur_backward",
    )(nat, slot, state, prior, keep, bound, gain, grad, pre, ext, inv)


def pin(*arrays):
    return [pltpu.with_memory_space_constraint(array, pltpu.HBM) for array in arrays]


def anywhere():
    return pl.BlockSpec(memory_space=pl.ANY)


def part_of(rows, cols, first):
    return pl.BlockSpec((pl.Element(rows), pl.Element(cols)), lambda i: (first, 0))


def pre_kernel(gain_ref, *refs, count):
    blocks, weights = refs[:count], refs[count : count + 3]
    rows_ref, normed_ref, pre_ref, out_w_ref = refs[-4:]
    blk = rows_ref.shape[0] // count
    more = blocks[0].shape[0] - blk
    chans = weights[0].shape[1]
    gain = gain_ref[...]
    for b, block in enumerate(blocks):

        def chunk(step, _, block=block, b=b):
            at = pl.multiple_of(step * 16, 16)
            value = block[pl.ds(at, 16), :]
            out = pl.ds(pl.multiple_of(b * blk + at, 16), 16)
            rows_ref[out, :] = value
            rows = value.astype(F32)
            normed_ref[out, :] = (rows * inverse_rms(rows) * gain).astype(BF16)
            return 0

        lax.fori_loop(0, blk // 16, chunk, 0, unroll=4)
        out_w_ref[b * more : (b + 1) * more, :] = block[blk:, :]
    for k, weight in enumerate(weights):
        pre_ref[:, k * chans : (k + 1) * chans] = dot_nn(normed_ref[...], weight[...])


def make_pre(gain, blocks, weights, held, blk, lo, size, out_lo, out_size):
    both, width = blocks[0].shape
    count = len(blocks)
    rows, more = blk * count, both - blk
    chans = weights[0].shape[1]
    out = jax.ShapeDtypeStruct
    inputs = 4 + count
    there = [k for k, array in enumerate(held) if array is not None]
    return pl.pallas_call(
        functools.partial(pre_kernel, count=count),
        grid=(1,),
        out_shape=(
            pltpu.HBM((size * blk, width), BF16),
            pltpu.HBM((size * blk, width), BF16),
            pltpu.HBM((size * blk, 3 * chans), F32),
            pltpu.HBM((out_size * more, width), BF16),
        ),
        in_specs=[vmem()] * inputs + [anywhere()] * len(there),
        out_specs=(
            part_of(rows, width, lo * blk),
            part_of(rows, width, lo * blk),
            part_of(rows, 3 * chans, lo * blk),
            part_of(more * count, width, (lo - out_lo) * more),
        ),
        input_output_aliases={inputs + n: k for n, k in enumerate(there)},
        compiler_params=params([((rows, width), 2)] * 6 + [((width + 4 * rows, 3 * chans), 2)]),
        cost_estimate=cost(6 * rows * width * chans, rows * width * 6 + 6 * width * chans),
        name="make_pre",
    )(gain, *blocks, *weights, *pin(*(held[k] for k in there)))


def back_kernel(weight_ref, *refs, count):
    blocks, (rows_ref, out_ref) = refs[:count], refs[-2:]
    blk = blocks[0].shape[0]
    for b, block in enumerate(blocks):
        rows_ref[b * blk : (b + 1) * blk, :] = block[...]
    out_ref[...] = dot_nt(rows_ref[...], weight_ref[...])


def make_back(weight, blocks, held, first, total):
    blk, width = blocks[0].shape
    rows, units = blk * len(blocks), weight.shape[0]
    out = jax.ShapeDtypeStruct
    count = 1 + len(blocks)
    return pl.pallas_call(
        functools.partial(back_kernel, count=len(blocks)),
        grid=(1,),
        out_shape=(pltpu.HBM((total, width), BF16), pltpu.HBM((total, units), F32)),
        in_specs=[vmem()] * count + [anywhere()] * len(held),
        out_specs=(part_of(rows, width, first), part_of(rows, units, first)),
        input_output_aliases={count + k: k for k in range(len(held))},
        compiler_params=params([((2 * rows + units, width), 2), ((rows, units), 4)] * 2),
        cost_estimate=cost(2 * rows * width * units, (rows + units) * width * 2),
        name="make_back",
    )(weight, *blocks, *pin(*held))


def gated_grad_kernel(weight_ref, *refs, count):
    blocks, (rows_ref, out_ref, ext_ref) = refs[:count], refs[-3:]
    blk = blocks[0].shape[0]
    width = rows_ref.shape[1]
    for b, block in enumerate(blocks):
        rows_ref[b * blk : (b + 1) * blk, :] = block[:, :width]
        ext_ref[b * blk : (b + 1) * blk, :] = block[:, width:]
    out_ref[...] = dot_nt(rows_ref[...], weight_ref[...])


def make_gated_grad(weight, blocks, held, first, total):
    chans, width = weight.shape
    blk = blocks[0].shape[0]
    rows = blk * len(blocks)
    out = jax.ShapeDtypeStruct
    count = 1 + len(blocks)
    return pl.pallas_call(
        functools.partial(gated_grad_kernel, count=len(blocks)),
        grid=(1,),
        out_shape=(pltpu.HBM((total, width), BF16), pltpu.HBM((total, chans), F32), pltpu.HBM((total, EXT), BF16)),
        in_specs=[vmem()] * count + [anywhere()] * len(held),
        out_specs=(
            part_of(rows, width, first),
            part_of(rows, chans, first),
            part_of(rows, EXT, first),
        ),
        input_output_aliases={count + k: k for k in range(len(held))},
        compiler_params=params([((2 * rows + chans, width + EXT), 2), ((rows, chans), 4)] * 2),
        cost_estimate=cost(2 * rows * width * chans, (rows + chans) * width * 2, scale=0),
        name="make_gated_grad",
    )(weight, *blocks, *pin(*held))


def mix_kernel(at_ref, nat_ref, w_a, w_b, w_c, w_d, *refs, count, held):
    gated, (out_ref, weight_s, gated_s) = refs[:count], refs[-3:]
    chans = gated[0].shape[1]
    rows = chans // 4

    @pl.when(pl.program_id(0) == 0)
    def _():
        for k in range(count):
            for part, weight in enumerate((w_a, w_b, w_c, w_d)):
                to = pl.multiple_of(k * chans + at_ref[part] * rows, rows)
                weight_s[pl.ds(to, rows), :] = weight[k * rows : (k + 1) * rows, :]

    for k in range(count):
        gated_s[:, k * chans : (k + 1) * chans] = gated[k][...]
    tile = 512
    for col in range(0, out_ref.shape[1], tile):
        summed = dot_nn(gated_s[...], weight_s[:, col : col + tile])
        if held:
            summed += refs[count][:, col : col + tile]
        out_ref[:, col : col + tile] = summed


def make_mix(nat, at, gated, weights, held, blk):
    count = len(gated)
    chans = gated[0].shape[1]
    width = weights[0].shape[1]
    nblk = nat.shape[0]
    whole = pl.BlockSpec(weights[0].shape, lambda i, at, nat: (0, 0), pipeline_mode=pl.Buffered(1))
    rows = pl.BlockSpec((blk, width), lambda i, at, nat: (i, 0))
    more = [] if held is None else [held]
    return pl.pallas_call(
        functools.partial(mix_kernel, count=count, held=bool(more)),
        out_shape=pltpu.HBM((nblk * blk, width), F32),
        grid_spec=pltpu.PrefetchScalarGridSpec(
            num_scalar_prefetch=2,
            grid=(nblk,),
            in_specs=[whole] * 4
            + [pl.BlockSpec((blk, chans), lambda i, at, nat: (nat[i], 0))] * count
            + [rows] * len(more),
            out_specs=rows,
            scratch_shapes=[
                pltpu.VMEM((count * chans, width), BF16),
                pltpu.VMEM((blk, count * chans), BF16),
            ],
        ),
        input_output_aliases={6 + count: 0} if more else {},
        compiler_params=params(
            [(weights[0].shape, 2)] * 4
            + [((count * chans, width), 2), ((blk, count * chans), 2)]
            + [((blk, chans), 2)] * (2 * count)
            + [((blk, width), 4)] * 5
        ),
        cost_estimate=cost(
            2 * nblk * blk * count * chans * width,
            count * chans * width * 2 + nblk * blk * (width * 4 + count * chans * 2),
        ),
        name="make_mix",
    )(at, nat, *weights, *gated, *pin(*more))


def glu_kernel(
    nat_ref, at_ref, gated_ref, w_a, w_b, w_c, w_d, mixed_ref, rows_ref, square_ref, gain_ref,
    gate_w_ref, up_w_ref, back_ref, *refs, first, count,
):
    normed_ref, hidden_ref, grad_gate_ref, grad_up_ref, inv_ref, term_ref, *own = refs[count:]
    step = pl.program_id(0)
    blk, width = rows_ref.shape
    *own, weight_s = own

    @pl.when(step == 0)
    def _():
        for part, weight in enumerate((w_a, w_b, w_c, w_d)):
            size = weight.shape[0]
            weight_s[pl.ds(pl.multiple_of(at_ref[part] * size, size), size), :] = weight[...]

    square = square_ref[pl.ds(nat_ref[first + step], 1), :]
    row = lax.broadcasted_iota(jnp.int32, (blk, blk), 0)
    col = lax.broadcasted_iota(jnp.int32, (blk, blk), 1)
    square = jnp.sum(jnp.where(row == col, square, 0.0), axis=1, keepdims=True)
    inv = lax.rsqrt(square / width + EPS)
    mixed = mixed_ref[...] + dot_nn(gated_ref[...], weight_s[...])
    middle = rows_ref[...].astype(F32) + mixed * inv
    inv_two = inverse_rms(middle)
    normed_ref[...] = (middle * inv_two * gain_ref[...]).astype(BF16)
    lane = lax.broadcasted_iota(jnp.int32, (blk, EXT), 1)
    inv_ref[...] = jnp.where(lane == 0, inv, jnp.where(lane == 1, inv_two, 0.0))
    if own:

        @pl.when(step == 0)
        def _():
            own[0][...] = middle

    gate = dot_nt(normed_ref[...], gate_w_ref[...])
    up = dot_nt(normed_ref[...], up_w_ref[...])
    back = back_ref[...]
    sig = jax.nn.sigmoid(gate)
    act = gate * sig
    hidden_ref[...] = (act * up).astype(BF16)
    grad_gate_ref[...] = (back * up * (sig * (1.0 + gate * (1.0 - sig)))).astype(BF16)
    grad_up_ref[...] = (back * act).astype(BF16)
    term_ref[...] = (
        dot_nn(grad_gate_ref[...], gate_w_ref[...]) + dot_nn(grad_up_ref[...], up_w_ref[...])
    ).astype(BF16)


def make_glu(nat, at, gated, weights, mixed, rows, square, gain, gate_w, up_w, back, held, lo, hi):
    total, width = rows.shape
    blk = square.shape[1]
    chans, units = gated.shape[1], gate_w.shape[0]
    out = jax.ShapeDtypeStruct

    def fixed(value):
        return pl.BlockSpec(
            value.shape, lambda i, nat, at: (0,) * value.ndim, pipeline_mode=pl.Buffered(1)
        )

    def tiled(cols, base=lo):
        return pl.BlockSpec((blk, cols), lambda i, nat, at: (base + i, 0))

    shapes = [pltpu.HBM((total, width), BF16)] + [pltpu.HBM((total, units), BF16)] * 3
    shapes += [pltpu.HBM((total, EXT), F32), out(((hi - lo) * blk, width), BF16)]
    specs = [tiled(width)] + [tiled(units)] * 3 + [tiled(EXT), tiled(width, 0)]
    if lo == 0:
        shapes.append(out((blk, width), F32))
        specs.append(pl.BlockSpec((blk, width), lambda i, nat, at: (0, 0)))
    return pl.pallas_call(
        functools.partial(glu_kernel, first=lo, count=len(held)),
        out_shape=shapes,
        grid_spec=pltpu.PrefetchScalarGridSpec(
            num_scalar_prefetch=2,
            grid=(hi - lo,),
            in_specs=[pl.BlockSpec((blk, chans), lambda i, nat, at: (nat[lo + i], 0))]
            + [pl.BlockSpec((chans // 4, width), lambda i, nat, at: (2, 0))] * 4
            + [tiled(width), tiled(width), fixed(square), fixed(gain)]
            + [fixed(gate_w), fixed(up_w), tiled(units)]
            + [anywhere()] * len(held),
            out_specs=specs,
            scratch_shapes=[pltpu.VMEM((chans, width), BF16)],
        ),
        input_output_aliases={14 + k: k for k in range(len(held))},
        compiler_params=params(
            [((chans, width), 2)] * 3
            + [(gate_w.shape, 2)] * 2
            + [((blk, width), 4)] * 12
            + [((blk, units), 4)] * 10
        ),
        cost_estimate=cost(
            (hi - lo) * blk * width * (2 * chans + 8 * units),
            (hi - lo) * blk * width * 8 + 4 * units * width,
        ),
        name="make_glu",
    )(nat, at, *pin(gated, *weights, mixed, rows), square, gain, gate_w, up_w, *pin(back, *held))


def matmul_kernel(lhs_ref, rhs_ref, out_ref):
    out_ref[...] = dot_nn(lhs_ref[...], rhs_ref[...]).astype(out_ref.dtype)


def make_product(lhs, rhs, blk, lo, hi):
    inner, width = rhs.shape
    rows = (hi - lo) * blk
    return pl.pallas_call(
        matmul_kernel,
        grid=(hi - lo,),
        out_shape=jax.ShapeDtypeStruct((rows, width), BF16),
        in_specs=[
            pl.BlockSpec((blk, inner), lambda i: (lo + i, 0)),
            pl.BlockSpec((inner, width), lambda i: (0, 0), pipeline_mode=pl.Buffered(1)),
        ],
        out_specs=pl.BlockSpec((blk, width), lambda i: (i, 0)),
        compiler_params=params([((inner, width), 2)] + [((blk, width + inner), 4)] * 5),
        cost_estimate=cost(2 * rows * inner * width, (rows * inner + (rows + inner) * width) * 2, scale=0),
        name="make_product",
    )(lhs, rhs)


def last_kernel(gpre_ref, w_a, w_b, w_c, normed_ref, term_ref, sum_ref):
    chans = w_a.shape[1]
    total = None
    for k, weight in enumerate((w_a, w_b, w_c)):
        term = dot_nt(gpre_ref[:, k * chans : (k + 1) * chans], weight[...])
        total = term if total is None else total + term
    term_ref[...] = total.astype(BF16)
    part = jnp.sum(total * normed_ref[...].astype(F32), axis=0, keepdims=True)

    @pl.when(pl.program_id(0) == 0)
    def _():
        sum_ref[...] = jnp.zeros_like(sum_ref)

    sum_ref[...] += part


def make_last(gpre, weights, normed, blk, lo, hi):
    width, chans = weights[0].shape
    rows = (hi - lo) * blk
    out = jax.ShapeDtypeStruct
    fixed = pl.BlockSpec((width, chans), lambda i: (0, 0), pipeline_mode=pl.Buffered(1))
    return pl.pallas_call(
        last_kernel,
        grid=(hi - lo,),
        out_shape=(out((rows, width), BF16), out((1, width), F32)),
        in_specs=[pl.BlockSpec((blk, 3 * chans), lambda i: (lo + i, 0))]
        + [fixed] * 3
        + [pl.BlockSpec((blk, width), lambda i: (lo + i, 0))],
        out_specs=(
            pl.BlockSpec((blk, width), lambda i: (i, 0)),
            pl.BlockSpec((1, width), lambda i: (0, 0)),
        ),
        compiler_params=params([((width, chans), 2)] * 3 + [((blk, width), 4)] * 8),
        cost_estimate=cost(6 * rows * width * chans, rows * width * 4 + 6 * width * chans),
        name="make_last",
    )(gpre, *weights, normed)


def middle_grad_kernel(
    r_ref, l_ref, part_ref, rows_ref, middle_ref, inv_ref, cot_ref, weight_ref, gain_ref,
    grad_ref, send_ref, gain_sum_ref,
):
    blk, width = rows_ref.shape
    gain = gain_ref[...]
    weight = weight_ref[0, 0]

    def chunk(step, summed):
        rows = pl.ds(pl.multiple_of(step * 16, 16), 16)
        grad_two = (
            r_ref[rows, :].astype(F32) + l_ref[rows, :].astype(F32) + part_ref[rows, :].astype(F32)
        )
        inv_two = inv_ref[rows, 1:2]
        middle = middle_ref[rows, :]
        unit = middle * inv_two
        scaled = grad_two * gain
        mean = jnp.mean(scaled * unit, axis=1, keepdims=True)
        grad = cot_ref[rows, :].astype(F32) * weight + inv_two * (scaled - unit * mean)
        grad_ref[rows, :] = grad
        sent = grad.astype(BF16)
        send_ref[rows, :width] = sent
        mix = middle - rows_ref[rows, :].astype(F32)
        inner = jnp.sum(sent.astype(F32) * mix, axis=1, keepdims=True)
        high, low = two_terms(inner)
        lane = lax.broadcasted_iota(jnp.int32, (16, EXT), 1)
        ext = jnp.where(
            lane == 0, high.astype(F32), jnp.where(lane == 1, low.astype(F32), 0.0)
        )
        send_ref[rows, width:] = ext.astype(BF16)
        return summed + jnp.sum(grad_two * unit, axis=0, keepdims=True)

    gain_sum_ref[...] = lax.fori_loop(0, blk // 16, chunk, jnp.zeros((1, width), F32))


def make_middle_grad(r_in, l_in, part, rows, middle, inv, cot, weight, gain):
    blk, width = rows.shape
    out = jax.ShapeDtypeStruct
    return pl.pallas_call(
        middle_grad_kernel,
        grid=(1,),
        out_shape=(
            out((blk, width), F32),
            out((blk, width + EXT), BF16),
            out((1, width), F32),
        ),
        in_specs=[vmem(), vmem(), pl.BlockSpec((blk, width), lambda i: (0, 0))]
        + [vmem()] * 2
        + [pl.BlockSpec((blk, EXT), lambda i: (0, 0)), vmem()]
        + [smem(), vmem()],
        out_specs=(vmem(),) * 3,
        compiler_params=params([((blk, width + EXT), 4)] * 6),
        cost_estimate=cost(blk * width * 16, blk * width * 20, scale=0),
        name="make_middle_grad",
    )(r_in, l_in, part, rows, middle, inv, cot, weight, gain)


def final_kernel(
    r_ref, l_ref, part_ref, rows_ref, grad_ref, gain_ref, out_ref,
):
    blk = rows_ref.shape[0]
    gain = gain_ref[...]

    def chunk(step, _):
        at = pl.multiple_of(step * 16, 16)
        rows = pl.ds(at, 16)
        grad = (
            r_ref[rows, :].astype(F32) + l_ref[rows, :].astype(F32) + part_ref[rows, :].astype(F32)
        )
        own = rows_ref[rows, :].astype(F32)
        inv = inverse_rms(own)
        unit = own * inv
        scaled = grad * gain
        mean = jnp.mean(scaled * unit, axis=1, keepdims=True)
        out_ref[rows, :] = grad_ref[rows, :] + inv * (scaled - unit * mean)
        return 0

    lax.fori_loop(0, blk // 16, chunk, 0)


def make_final(r_in, l_in, part, rows, grad, gain):
    blk, width = rows.shape
    return pl.pallas_call(
        final_kernel,
        out_shape=jax.ShapeDtypeStruct((blk, width), F32),
        in_specs=[vmem()] * 6,
        out_specs=vmem(),
        compiler_params=params([((blk, width), 4)] * 8),
        cost_estimate=cost(blk * width * 16, blk * width * 18),
        name="make_final",
    )(r_in, l_in, part, rows, grad, gain)


class Ring:
    def __init__(self, size):
        self.size = size
        self.steps = size // 2
        order = list(range(0, size, 2)) + list(range(size - 1, 0, -2))
        place = {device: at for at, device in enumerate(order)}
        self.right = [(order[i], order[(i + 1) % size]) for i in range(size)]
        self.left = [(b, a) for a, b in self.right]
        offs = [0]
        for k in range(1, self.steps):
            offs += [-k, k]
        offs.append(self.steps)
        cuts = [0, *range(3, size, 2), size]
        self.spans = list(zip(cuts[:-1], cuts[1:]))
        self.pairs = [(0, 1), (1, 3), *self.spans[1:]]
        nat = np.zeros((size, size), np.int32)
        slot = np.zeros((size, size), np.int32)
        for device in range(size):
            for at, off in enumerate(offs):
                block = order[(place[device] + off) % size]
                nat[device, at] = block
                slot[device, block] = at
        self.nat, self.slot = nat, slot

    def move(self, right, left):
        return lax.ppermute(right, "mp", self.right), lax.ppermute(left, "mp", self.left)

    def gather(self, k, pair):
        right, left = pair
        if k == self.steps - 1:
            rows = right.shape[0] // 32 * 16
            return self.move(right[:rows], left[rows:])
        return self.move(right, left)

    def scatter(self, k, pair, group):
        if k == 0:
            rows = group.shape[0] // 2
            return self.move(group[:rows], group[rows:])
        right, left = pair
        blk = group.shape[0] // 2
        to_left, to_right = group[:blk], group[blk:]
        if k == 1:
            rows = blk // 2
            right = jnp.concatenate([add(right, to_right[:rows]), to_right[rows:]], axis=0)
            left = jnp.concatenate([to_left[:rows], add(left, to_left[rows:])], axis=0)
        else:
            right, left = add(right, to_right), add(left, to_left)
        return self.move(right, left)


def close(*values):
    return lax.optimization_barrier(values)


def add(a, b):
    return (a.astype(F32) + b.astype(F32)).astype(BF16)


def dp_swap(value, bit):
    return lax.ppermute(value, "dp", [(i, i ^ bit) for i in range(lax.axis_size("dp"))])


def mp_swap(value, bit):
    return lax.ppermute(value, "mp", [(i, i ^ bit) for i in range(lax.axis_size("mp"))])


def local(
    block_input,
    out_cotangent,
    segments,
    domain_tags,
    counts,
    attn_gain,
    mlp_gain,
    norm_gain,
    bound_table,
    w_input,
    w_forget,
    w_gate_mix,
    w_out,
    w_glu_gate,
    w_glu_up,
    w_glu_down,
):
    blk, width = block_input.shape
    chans = w_input.shape[1]
    seqs = segments.shape[0]
    total = seqs * LEN
    mp_size, dp_size = lax.axis_size("mp"), lax.axis_size("dp")
    mp_index, dp_index = lax.axis_index("mp"), lax.axis_index("dp")
    ring = Ring(mp_size)
    spans, steps = ring.spans, ring.steps
    last = steps - 1
    nat = lax.dynamic_index_in_dim(jnp.asarray(ring.nat), mp_index, 0, keepdims=False)
    slot = lax.dynamic_index_in_dim(jnp.asarray(ring.slot), mp_index, 0, keepdims=False)
    at = dp_index ^ jnp.array([0, 2, 1, 3], jnp.int32)

    lanes = -(-chans // 128) * 128
    pad = lanes - chans

    def pad_cols(array):
        return jnp.pad(array, ((0, 0), (0, pad))) if pad else array

    mix_weights = [pad_cols(w_input), pad_cols(w_forget), pad_cols(w_gate_mix)]
    w_out_pad = jnp.pad(w_out, ((0, pad), (0, 0))) if pad else w_out
    attn_row, mlp_row = attn_gain[None, :], mlp_gain[None, :]
    gate_w, up_w = w_glu_gate.T, w_glu_up.T

    layer_ids = jnp.arange(NLAYER)
    pick = ((layer_ids >= 1) & (layer_ids <= LAYER)).astype(F32)[:, None]
    bound = pad_cols(jnp.sum(jax.nn.softmax(bound_table, axis=0) * pick, axis=0)[None, :])
    gain = pad_cols(norm_gain[None, :])
    keep = jnp.concatenate(
        [jnp.zeros((seqs, 1), F32), (segments[:, 1:] == segments[:, :-1]).astype(F32)], axis=1
    ).reshape(total, 1)
    seq_count = jnp.sum(
        jnp.where(
            domain_tags[:, None] == jnp.arange(NDOM)[None, :], counts.astype(F32)[None, :], 0.0
        ),
        axis=1,
    )
    weight = lax.dynamic_slice_in_dim(lax.rsqrt(seq_count), mp_index * blk // LEN, 1, 0)
    grad_b = (out_cotangent.astype(F32) * weight[:, None]).astype(BF16)


    quarter = lax.dynamic_slice_in_dim(w_out_pad, dp_index * (lanes // 4), lanes // 4, axis=0)
    own = jnp.concatenate([block_input, quarter], axis=0)
    pair, waiting, held = (own, own), [own], (None,) * 4
    table = bound_table[None]
    split = spans[last - 1][0]

    def pre_group(blocks, held, g):
        part = (split, mp_size - split) if spans[g][0] >= split else (0, split)
        return make_pre(attn_row, blocks, mix_weights, held, blk, spans[g][0], mp_size, *part)

    for k in range(steps):
        pair = ring.gather(k, pair)
        if k == 0:
            more = mp_swap(table, 1)
            pair, bound, keep, grad_b, nat, slot, at = close(
                pair, bound, keep, grad_b, nat, slot, at
            )
            waiting += pair
            continue
        held = pre_group(waiting, held, k - 1)
        if k == 1:
            pair, held, more = close(pair, held, more)
            table = jnp.concatenate([table, more], axis=0)
        elif k < last:
            if k == last - 1:
                *held, out_own = held
                near = [out_own, dp_swap(out_own, 2), dp_swap(out_own, 1)]
                more = mp_swap(table, 2)
                pair, held, near[2], grad_b = close(pair, held, near[2], grad_b)
                held = (*held, None)
            else:
                pair, held = close(pair, held)
        else:
            cot = ring.gather(0, (grad_b, grad_b))
            pair, held, more, near[1] = close(pair, held, more, near[1])
            table = jnp.concatenate([table, more], axis=0)
        waiting = list(pair) if k < last else [jnp.concatenate(pair, axis=0)]
    rows, normed, pre, out_own = pre_group(waiting, held, last)

    near.append(dp_swap(near[1], 1))
    far = [out_own, dp_swap(out_own, 2), dp_swap(out_own, 1)]
    state, prior, gated_own = recur_forward(nat, slot, pre, keep, bound, gain, blk)
    gated_own, cot = close(gated_own, cot)
    pair, gated_blocks, mixed = (gated_own, gated_own), [gated_own], None
    held, cot_waiting = (), [grad_b]
    for k in range(steps):
        pair = ring.gather(k, pair)
        if k == 0:
            pair, near, far[2], cot = close(pair, near, far[2], cot)
            cot_waiting += cot
        else:
            cot = ring.gather(k, cot)
            held = make_back(w_glu_down, cot_waiting, held, spans[k - 1][0] * blk, total)
            if k < last:
                if k == last - 1:
                    mixed = make_mix(nat, at, gated_blocks, near, None, blk)
                    pair, cot, held, mixed, far[1] = close(pair, cot, held, mixed, far[1])
                    far.append(dp_swap(far[1], 1))
                else:
                    pair, cot, held = close(pair, cot, held)
            else:
                mixed = make_mix(nat, at, gated_blocks[split:], far, mixed, blk)
                pair, cot, held, mixed = close(pair, cot, held, mixed)
            cot_waiting = list(cot) if k < last else [jnp.concatenate(cot, axis=0)]
        gated_blocks += pair if k < last else [jnp.concatenate(pair, axis=0)]
    cot_all, back = make_back(w_glu_down, cot_waiting, held, spans[last][0] * blk, total)
    squares = sum(block[total:, :128].astype(F32) for block in gated_blocks)
    squares = squares[:mp_size] + squares[mp_size:]

    pairs = ring.pairs

    def glu_group(held, g):
        weights = pin(gate_w, up_w) if g in (0, last - 1) else (gate_w, up_w)
        return make_glu(
            nat, at, gated_blocks[-1], far, mixed, rows, squares, mlp_row, *weights,
            back, held, *pairs[g],
        )

    def out_group(g):
        return make_product(hidden, w_glu_down, blk, *pairs[g])

    made = glu_group((), steps)
    held, term = made[:5], made[5]
    for k in range(steps):
        pair = ring.scatter(k, pair, term)
        made = glu_group(held, last - k)
        held, term = made[:5], made[5]
        if 4 << k < mp_size:
            more = mp_swap(table, 4 << k)
            pair, held, term, more = close(pair, held, term, more)
            table = jnp.concatenate([table, more], axis=0)
        elif k == last - 1:
            table = jnp.take(table, jnp.arange(mp_size) ^ mp_index, axis=0)
            shares = jax.nn.softmax(table.transpose(1, 0, 2).reshape(NLAYER, width), axis=0)
            pair, held, term, shares = close(pair, held, term, shares)
        else:
            pair, held, term = close(pair, held, term)
    two, hidden, grad_gate, grad_up, inv = held
    middle = made[6]
    outs = [None] * (steps + 1)
    outs[steps] = out_group(steps)
    grad_middle, sent, mlp_term = make_middle_grad(
        *pair, term, block_input, middle, inv, out_cotangent, weight[:, None], mlp_row
    )

    size = width // dp_size

    def cols(array, bits):
        return lax.dynamic_slice_in_dim(array, (dp_index ^ bits) * size, size, axis=1)

    def far_slice(own, rest):
        return (own[0] + rest[0].astype(F32)).astype(BF16)

    def slice_sum(own, rest, far):
        return own[1] + rest[1].astype(F32) + far.astype(F32)

    def slices(left, right, which, split_left=False):
        found = []
        for bits in ((3, 1) if which == "rest" else (2, 0)):
            if split_left:
                found.append(dot_tn(cols(left, bits), right))
            else:
                found.append(dot_tn(left, cols(right, bits)))
        return jnp.stack([value.astype(BF16) for value in found]) if which == "rest" else found

    sent, hidden, two, cot_all, grad_gate, grad_up = close(
        sent, hidden, two, cot_all, grad_gate, grad_up
    )
    pair, res, sent_waiting, held = (sent, sent), (), [sent], ()
    for k in range(steps):
        pair = ring.gather(k, pair)
        res = ring.scatter(k, res, outs[steps - k])
        outs[last - k] = out_group(last - k)
        if k:
            held = make_gated_grad(w_out_pad, sent_waiting, held, spans[k - 1][0] * blk, total)
        if k == 0:
            down = slices(hidden, cot_all, "rest"), slices(hidden, cot_all, "own")
            pair, res, outs[last], down, two, hidden = close(
                pair, res, outs[last], down, two, hidden
            )
            sent_waiting += pair
            continue
        if k == 1:
            down_rest = dp_swap(down[0], 1)
            gate = slices(grad_gate, two, "rest"), slices(grad_gate, two, "own")
            pair, res, outs, held, down_rest, gate, two, hidden = close(
                pair, res, outs, held, down_rest, gate, two, hidden
            )
        elif k == 2:
            down_far = dp_swap(far_slice(down[1], down_rest), 2)
            gate_rest = dp_swap(gate[0], 1)
            up = slices(grad_up, two, "rest"), slices(grad_up, two, "own")
            pair, res, outs, held, gate_rest, up, hidden = close(
                pair, res, outs, held, gate_rest, up, hidden
            )
        elif k < last:
            pair, res, outs, held = close(pair, res, outs, held)
        if k == last:
            up_rest = dp_swap(up[0], 1)
            pair, held, up_rest, outs[0] = close(pair, held, up_rest, outs[0])
        sent_waiting = list(pair) if k < last else [jnp.concatenate(pair, axis=0)]
    sent_all, grad, ext = make_gated_grad(
        w_out_pad, sent_waiting, held, spans[last][0] * blk, total
    )

    grad_pre, gated, norm_term, bound_grad = recur_backward(
        nat, slot, grad, pre, ext, inv, state, prior, keep, bound, gain, blk, width
    )

    def last_group(g, grad_pre):
        return make_last(grad_pre, mix_weights, normed, blk, *pairs[g])

    def placed(row):
        wide = jnp.zeros((1, width), F32)
        return lax.dynamic_update_slice(wide, row[:, :chans], (0, mp_index * chans))

    lasts = [None] * (steps + 1)
    lasts[steps] = last_group(steps, grad_pre)
    for k in range(steps):
        pair = ring.scatter(k, pair, lasts[steps - k][0])
        if k == 0:
            gate_far = dp_swap(far_slice(gate[1], gate_rest), 2)
            lasts[last] = last_group(last, grad_pre)
            mix_rest = slices(normed, grad_pre, "rest", True)
            pair, res, lasts[last], mix_rest, grad_pre, normed, gated, sent_all, down_far, up = close(
                pair, res, lasts[last], mix_rest, grad_pre, normed, gated, sent_all, down_far, up
            )
        elif k == 1:
            mix_rest = dp_swap(mix_rest, 1)
            up_far = dp_swap(far_slice(up[1], up_rest), 2)
            for g in range(last):
                lasts[g] = last_group(g, grad_pre)
            mix = slices(normed, grad_pre, "own", True)
            down, res, outs[0] = close(down, res, outs[0])
            pair, lasts, mix_rest, mix, gated, sent_all, gate_far, down, res, up = close(
                pair, lasts, mix_rest, mix, gated, sent_all, gate_far, down, res, up
            )
        elif k == 2:
            mix_far = dp_swap(far_slice(mix, mix_rest), 2)
            out = slices(gated, sent_all, "rest"), slices(gated, sent_all, "own")
            down_grad = slice_sum(down[1], down_rest, down_far)
            result = (
                middle + res[0].astype(F32) + res[1].astype(F32) + outs[0].astype(F32)
            ).astype(BF16)

            attn_term = sum(found[1] for found in lasts) / attn_row
            packed = jnp.concatenate(
                [attn_term, mlp_term, placed(norm_term), placed(bound_grad)], axis=0
            ).reshape(-1, 128)
            packed = packed + dp_swap(packed, 1)
            packed = packed + mp_swap(packed, 1)
            pair, out, down_grad, result, packed, gate, up, up_far = close(
                pair, out, down_grad, result, packed, gate, up, up_far
            )
        elif k < last:
            (pair,) = close(pair)
        else:
            out_rest = dp_swap(out[0], 1)
            reach = 2
            while reach < mp_size:
                packed = packed + mp_swap(packed, reach)
                reach *= 2
            glu_gate_grad = slice_sum(gate[1], gate_rest, gate_far)
            glu_up_grad = slice_sum(up[1], up_rest, up_far)
            pair, packed, out_rest, glu_gate_grad, glu_up_grad, mix_far = close(
                pair, packed, out_rest, glu_gate_grad, glu_up_grad, mix_far
            )
    out_far = dp_swap(far_slice(out[1], out_rest), 2)
    packed = packed + dp_swap(packed, 2)
    grad_block_input = make_final(*pair, lasts[0][0], block_input, grad_middle, attn_row)
    mix_grad = slice_sum(mix, mix_rest, mix_far)
    out_grad = slice_sum(out[1], out_rest, out_far)[:chans]
    glu_gate_grad, glu_up_grad = glu_gate_grad.T, glu_up_grad.T

    attn_sum, mlp_sum, norm_sum, bound_sum = packed.reshape(4, width)
    pick_grad = pick * bound_sum[None, :]
    table_sum = shares * (pick_grad - jnp.sum(shares * pick_grad, axis=0, keepdims=True))
    return (
        result,
        grad_block_input,
        attn_sum,
        mlp_sum,
        norm_sum,
        table_sum,
        mix_grad[:, :chans],
        mix_grad[:, lanes : lanes + chans],
        mix_grad[:, 2 * lanes : 2 * lanes + chans],
        out_grad,
        glu_gate_grad,
        glu_up_grad,
        down_grad,
    )


def solution(mesh):
    placed = (
        P(("dp", "mp"), None),
        P(("dp", "mp"), None),
        P("dp", None),
        P("dp"),
        P(),
        P(),
        P(),
        P("mp"),
        P(None, "mp"),
        P(None, "mp"),
        P(None, "mp"),
        P(None, "mp"),
        P("mp", None),
        P(None, "mp"),
        P(None, "mp"),
        P("mp", None),
    )
    return jax.shard_map(
        local,
        mesh=mesh,
        in_specs=placed,
        out_specs=(
            P(("dp", "mp"), None),
            P(("dp", "mp"), None),
            P(),
            P(),
            P(),
            P(),
            P("dp", "mp"),
            P("dp", "mp"),
            P("dp", "mp"),
            P("mp", "dp"),
            P("dp", "mp"),
            P("dp", "mp"),
            P("mp", "dp"),
        ),
        check_vma=False,
    )
```
